256 devices in a mesh: row: 8 (over x, y_hi), grp: 32 (over z, y_lo, core).
Axes of the slice: x: 4, y: 4 (y_hi: 2, y_lo: 2; y = y_hi * 2 + y_lo), z: 8, core: 2. Of those that a mesh axis runs over, the one named last changes fastest.
Arguments:
- segments: bfloat16 [32, 128, 128, 512], P('grp', 'row'), may hold values from -40 to 40
- conv_weight: bfloat16 [3, 512, 512], replicated, may hold values from -0.15625 to 0.15625
- gain: float32 [512], replicated, may hold values from 0.1 to 1.9
- head: bfloat16 [512, 128], replicated, may hold values from -0.25 to 0.25
- group: int32 [32, 128], P('grp', 'row'), may hold values from 0 to 7
- positive: int32 [32, 128], P('grp', 'row'), may hold values from 0 to 127, as said below
Outputs:
- grad_conv: float32 [3, 512, 512], replicated
- grad_gain: float32 [512], replicated
- projector_derivative: float32 [512, 128], replicated
The draws below stay inside these ranges and needn't reach their ends.
Inputs may be any that keep to these rules, and one draw needn't show every extreme that they name: positive[c, i] is another segment of the same index c with the same group, and positive[c, positive[c, i]] == i.
All inputs are finite; a program needn't handle non-finite values.
Results may differ from the reference program's by a relative error of at most 0.003.
The reference program's roundings to bfloat16 on the way count: a program that leaves them out, or rounds other values in their place, can miss the bound.
Values sent between devices are 32-bit elements; how exact they have to be, the bound alone decides.
No kernel may reach another device: no remote copies, remote signals or barrier semaphores. Data moves between devices by JAX's collectives and lax.ppermute only.
A program may use at most 64 MiB of HBM per device.

```python
import math
from functools import partial
import jax
import jax.numpy as jnp
from jax import lax

C = 512
PROJ = 128
LEN = 128
KERNEL = 3
DILATION_GAP = 2
GROUPS = 8
ROWSEGS = 128
COLS = 32


def pair_layout(key):
    column_keys = jax.random.split(jax.random.fold_in(key, 101), COLS)
    orders = jax.vmap(lambda one_key: jax.random.permutation(one_key, ROWSEGS))(column_keys).astype(jnp.int32)
    slot_index = jnp.arange(ROWSEGS, dtype=jnp.int32)
    partner_slot = jnp.bitwise_xor(slot_index, 1)
    draw_one = jax.random.randint(jax.random.fold_in(key, 202), (COLS, ROWSEGS // 2), 0, GROUPS, dtype=jnp.int32)
    draw_two = jax.random.randint(jax.random.fold_in(key, 303), (COLS, ROWSEGS // 2), 0, GROUPS, dtype=jnp.int32)
    pair_group = jnp.minimum(draw_one, draw_two).at[:, 0].set(GROUPS - 1).at[:, 1].set(0)
    slot_group = jnp.repeat(pair_group, 2, axis=1)
    column_rows = jnp.arange(COLS, dtype=jnp.int32)[:, None]
    partner_ids = jnp.zeros((COLS, ROWSEGS), jnp.int32).at[column_rows, orders].set(orders[:, partner_slot])
    group_ids = jnp.zeros((COLS, ROWSEGS), jnp.int32).at[column_rows, orders].set(slot_group)
    return (group_ids, partner_ids)


def draw_group(key, part):
    return pair_layout(key)[0]


def draw_positive(key, part):
    return pair_layout(key)[1]


def draw_segments(key, part):
    shape = (COLS, ROWSEGS, LEN, C)
    row_scale = jnp.exp(jax.random.uniform(jax.random.fold_in(key, 11), (COLS, ROWSEGS, LEN, 1), jnp.float32, 0.0, math.log(10.0)))
    chan_scale = jnp.exp(jax.random.uniform(jax.random.fold_in(key, 12), (1, 1, 1, C), jnp.float32, 0.0, math.log(10.0)))
    base = jax.random.truncated_normal(jax.random.fold_in(key, 15), -4.0, 4.0, shape, jnp.float32)
    return (base * row_scale * chan_scale * 0.1).astype(jnp.bfloat16)


def gaussian(key, extent, width, most, held_as=jnp.bfloat16):
    return jnp.clip(width * jax.random.normal(key, extent, jnp.float32), -most, most).astype(held_as)


def setup_inputs(seed: int = 0) -> dict:
    key_list = jax.random.split(jax.random.key(seed), 7)
    return {
        "segments": draw_segments(jax.random.fold_in(key_list[6], 71), 0),
        "conv_weight": gaussian(key_list[1], (KERNEL, C, C), (KERNEL * C) ** -0.5, 0.15625),
        "gain": jnp.clip(1.0 + 0.18 * jax.random.normal(key_list[2], (C,), jnp.float32), 0.1, 1.9),
        "head": gaussian(key_list[3], (C, PROJ), C ** -0.5, 0.25),
        "group": draw_group(jax.random.fold_in(key_list[6], 71), 0),
        "positive": draw_positive(jax.random.fold_in(key_list[6], 71), 0),
    }


logit_divisor = 0.1

def unit_rows(values):
    return values * lax.rsqrt(lax.optimization_barrier(jnp.mean(values * values, axis=-1, keepdims=True)) + 1e-05)

def scale_embed(projected):
    return unit_rows(projected) * projected.shape[-1] ** (-0.5)

def filter_tap_window(normalized_rows, filter_tap_index, spacing):
    sequence_length = normalized_rows.shape[1]
    padded = jnp.pad(normalized_rows, ((0, 0), (spacing, spacing), (0, 0)))
    return padded[:, filter_tap_index * spacing:filter_tap_index * spacing + sequence_length]

def reverse_tap_gather(term, filter_tap_index, spacing):
    sequence_length = term.shape[1]
    padded = jnp.pad(term, ((0, 0), (spacing, spacing), (0, 0)))
    begin = (2 - filter_tap_index) * spacing
    return padded[:, begin:begin + sequence_length]

def encode(patient_piece_records, conv_weight, gain, head):
    inputs = patient_piece_records.astype(jnp.float32)
    unit = unit_rows(inputs)
    normalized_rows = (unit * gain).astype(jnp.bfloat16)
    segment_count, sequence_length, channel_count = normalized_rows.shape
    conv = jnp.zeros((segment_count * sequence_length, channel_count), jnp.float32)
    for filter_tap_index in range(conv_weight.shape[0]):
        shifted_input = filter_tap_window(normalized_rows, filter_tap_index, DILATION_GAP).reshape(segment_count * sequence_length, channel_count)
        conv = conv + jnp.dot(shifted_input, conv_weight[filter_tap_index], preferred_element_type=jnp.float32)
    conv = conv.reshape(segment_count, sequence_length, channel_count)
    hidden = inputs + jax.nn.gelu(conv, approximate=True)
    pooled = lax.optimization_barrier(jnp.mean(hidden, axis=1)).astype(jnp.bfloat16)
    projected = jnp.dot(pooled, head, preferred_element_type=jnp.float32)
    return (unit, normalized_rows, conv, pooled, projected)

def backward(embed_grad, unit, normalized_rows, conv, pooled, projected, conv_weight, head):
    projected_grad = jax.vjp(scale_embed, projected)[1](embed_grad)[0]
    projector_derivative = jnp.dot(pooled.astype(jnp.float32).T, projected_grad, precision=lax.Precision.HIGHEST)
    pooled_grad = jnp.dot(projected_grad, head.astype(jnp.float32).T, precision=lax.Precision.HIGHEST)
    segment_count, sequence_length, channel_count = conv.shape
    hidden_grad = jnp.broadcast_to(pooled_grad[:, None, :] / sequence_length, conv.shape)
    conv_grad = jax.vjp(partial(jax.nn.gelu, approximate=True), conv)[1](hidden_grad)[0].astype(jnp.bfloat16)
    flat_grad = conv_grad.reshape(segment_count * sequence_length, channel_count)
    tap_grads = []
    normalized_gradient = jnp.zeros((segment_count, sequence_length, channel_count), jnp.float32)
    for filter_tap_index in range(conv_weight.shape[0]):
        shifted_input = filter_tap_window(normalized_rows, filter_tap_index, DILATION_GAP).reshape(segment_count * sequence_length, channel_count)
        tap_grads.append(lax.dot_general(shifted_input, flat_grad, (((0,), (0,)), ((), ())), preferred_element_type=jnp.float32))
        backward_term = lax.dot_general(flat_grad, conv_weight[filter_tap_index], (((1,), (1,)), ((), ())), preferred_element_type=jnp.float32)
        normalized_gradient = normalized_gradient + reverse_tap_gather(backward_term.reshape(segment_count, sequence_length, channel_count), filter_tap_index, DILATION_GAP)
    grad_conv = jnp.stack(tap_grads)
    grad_gain = lax.optimization_barrier(jnp.sum(normalized_gradient * unit, axis=(0, 1)))
    return (grad_conv, grad_gain, projector_derivative)

def reference(segments, conv_weight, gain, head, group, positive):
    matrix_width_number, matrix_height_number = group.shape
    global_multiplier = (matrix_width_number * matrix_height_number) ** (-0.5) / logit_divisor

    def embed_column(column_data):
        return scale_embed(encode(column_data, conv_weight, gain, head)[4])
    embeddings = lax.map(embed_column, segments)

    def column_grad(packed):
        encounter_latent_vector, group_ids, partners = packed
        cosine_affinity_matrix = jnp.dot(encounter_latent_vector, encounter_latent_vector.T, precision=lax.Precision.HIGHEST) / logit_divisor
        positions = jnp.arange(matrix_height_number, dtype=jnp.int32)
        same_group = (group_ids[:, None] == group_ids[None, :]) & (positions[:, None] != positions[None, :])
        log_total = jnp.log(lax.optimization_barrier(jnp.sum(jnp.where(same_group, jnp.exp(cosine_affinity_matrix), 0.0), axis=1)))
        softmax = jnp.where(same_group, jnp.exp(cosine_affinity_matrix - log_total[:, None]), 0.0)
        row_term = jnp.dot(softmax, encounter_latent_vector, precision=lax.Precision.HIGHEST)
        column_term = jnp.dot(softmax.T, encounter_latent_vector, precision=lax.Precision.HIGHEST)
        return global_multiplier * (row_term + column_term - 2.0 * encounter_latent_vector[partners])
    embed_grads = lax.map(column_grad, (embeddings, group, positive))

    def accumulate(carry, packed):
        column_data, embed_grad = packed
        unit, normalized_rows, conv, pooled, projected = encode(column_data, conv_weight, gain, head)
        terms = backward(embed_grad, unit, normalized_rows, conv, pooled, projected, conv_weight, head)
        return ((carry[0] + terms[0], carry[1] + terms[1], carry[2] + terms[2]), None)
    start_value = (jnp.zeros(conv_weight.shape, jnp.float32), jnp.zeros(gain.shape, jnp.float32), jnp.zeros(head.shape, jnp.float32))
    totals, _ = lax.scan(accumulate, start_value, (segments, embed_grads))
    return (totals[0], totals[1], totals[2])
```

```python
import functools

import jax
import jax.numpy as jnp
from jax import lax
from jax.experimental import pallas as pl
from jax.experimental.pallas import tpu as pltpu
from jax.sharding import Mesh, PartitionSpec as P

GAP = 2
TEMPERATURE = 0.1
EPS = 1e-05
HIGHEST = lax.Precision.HIGHEST

SEGS = 16
LEN = 128
C = 512
PROJ = 128
TAPS = 3
STEP_SEGS = 4
ROWS = STEP_SEGS * LEN
STEPS = SEGS // STEP_SEGS

RANKS = 8
PLANE = 16
DEPTH = 8
BLOCKS = TAPS * C // 128
HALF = BLOCKS // 2
CONV_ROWS = HALF * (C // PLANE)
PROJ_ROWS = C // 2 // PLANE
CHUNK = CONV_ROWS + PROJ_ROWS
GAIN_ROWS = 8
Z_CONV = CONV_ROWS // DEPTH
Z_PROJ = PROJ_ROWS // DEPTH
Z_CHUNK = 32

VMEM = pltpu.VMEM
SMEM = pltpu.SMEM


def whole(shape, space=None):
    zeros = (0,) * len(shape)
    return pl.BlockSpec(shape, lambda *_: zeros, memory_space=space)


def later(rows):
    return jnp.concatenate([rows[GAP:], jnp.zeros((GAP, rows.shape[1]), rows.dtype)], axis=0)


def earlier(rows):
    return jnp.concatenate([jnp.zeros((GAP, rows.shape[1]), rows.dtype), rows[:-GAP]], axis=0)


def unit_rows(values):
    return values * lax.rsqrt(jnp.mean(values * values, axis=-1, keepdims=True) + EPS)


def forward_kernel(
    group, segments, weight, gain, head, normed_out, slope_out, pooled_out, projected_out, send_out, pooled
):
    step = pl.program_id(0)
    cubic = 0.044715
    scale = 0.7978845608028654
    for index in range(STEP_SEGS):
        inputs = segments[0, index].astype(jnp.float32)
        normed = (unit_rows(inputs) * gain[...]).astype(jnp.bfloat16)
        normed_out[index * LEN : (index + 1) * LEN, :] = normed
        conv = jnp.dot(earlier(normed), weight[0], preferred_element_type=jnp.float32)
        conv += jnp.dot(normed, weight[1], preferred_element_type=jnp.float32)
        conv += jnp.dot(later(normed), weight[2], preferred_element_type=jnp.float32)
        square = conv * conv
        bent = jnp.tanh(conv * (scale + (scale * cubic) * square))
        half = 0.5 + 0.5 * bent
        hidden = inputs + conv * half
        slope_out[index * LEN : (index + 1) * LEN, :] = half + (0.5 * conv) * (1.0 - bent * bent) * (
            scale + (3.0 * scale * cubic) * square
        )
        pooled[pl.ds(step * STEP_SEGS + index, 1), :] = jnp.sum(hidden, axis=0, keepdims=True) * (1.0 / LEN)

    @pl.when(step == STEPS - 1)
    def _():
        rounded = pooled[...].astype(jnp.bfloat16)
        pooled_out[...] = rounded
        projected = jnp.dot(rounded, head[...], preferred_element_type=jnp.float32)
        projected_out[...] = projected
        embedding = unit_rows(projected) * PROJ ** (-0.5)
        lane = lax.broadcasted_iota(jnp.int32, (8, 128), 1) & (SEGS - 1)
        groups = jnp.zeros((8, 128), jnp.int32)
        for index in range(SEGS):
            groups = jnp.where(lane == index, group[0, index], groups)
        groups = groups.astype(jnp.float32)
        for rank in range(RANKS):
            send_out[rank, 0:SEGS, :] = embedding
            send_out[rank, SEGS:, :] = groups


def forward(group, segments, weight, gain, head):
    f32 = jnp.float32
    return pl.pallas_call(
        forward_kernel,
        grid=(STEPS,),
        in_specs=[
            whole((1, SEGS), SMEM),
            pl.BlockSpec((1, STEP_SEGS, LEN, C), lambda i: (0, i, 0, 0)),
            whole((TAPS, C, C)),
            whole((1, C)),
            whole((C, PROJ)),
        ],
        out_specs=[
            pl.BlockSpec((ROWS, C), lambda i: (i, 0)),
            pl.BlockSpec((ROWS, C), lambda i: (i, 0)),
            whole((SEGS, C)),
            whole((SEGS, PROJ)),
            whole((RANKS, SEGS + 8, PROJ)),
        ],
        out_shape=[
            jax.ShapeDtypeStruct((SEGS * LEN, C), jnp.bfloat16),
            jax.ShapeDtypeStruct((SEGS * LEN, C), f32),
            jax.ShapeDtypeStruct((SEGS, C), jnp.bfloat16),
            jax.ShapeDtypeStruct((SEGS, PROJ), f32),
            jax.ShapeDtypeStruct((RANKS, SEGS + 8, PROJ), f32),
        ],
        scratch_shapes=[VMEM((SEGS, C), f32)],
        compiler_params=pltpu.CompilerParams(vmem_limit_bytes=48 << 20),
        cost_estimate=pl.CostEstimate(flops=2 * SEGS * LEN * TAPS * C * C, bytes_accessed=10 << 20, transcendentals=SEGS * LEN * C),
        name="forward",
    )(group, segments, weight, gain, head)


def loss_gradient(positive, gathered, projected, pooled, head, partner, place):
    embeddings = gathered[:, 0:SEGS, :].reshape(RANKS * SEGS, PROJ)
    own = unit_rows(projected[...]) * PROJ ** (-0.5)
    count = RANKS * SEGS
    nt = (((1,), (1,)), ((), ()))
    lane = lax.broadcasted_iota(jnp.int32, (8, 128), 1)
    groups = jnp.zeros((8, 128), jnp.float32)
    for rank in range(RANKS):
        groups = jnp.where(lane >> 4 == rank, gathered[rank, SEGS:, :], groups)
    by_column = jnp.broadcast_to(groups[0:1], (count, count))
    by_row = by_column.T
    row = lax.broadcasted_iota(jnp.int32, (count, count), 0)
    column = lax.broadcasted_iota(jnp.int32, (count, count), 1)
    same = (by_row == by_column) & (row != column)
    scores = lax.dot_general(
        embeddings, embeddings, nt, precision=HIGHEST, preferred_element_type=jnp.float32
    ) / TEMPERATURE
    column_total = jnp.log(jnp.sum(jnp.where(same, jnp.exp(scores), 0.0), axis=0, keepdims=True))

    own_scores = lax.dot_general(
        own, embeddings, nt, precision=HIGHEST, preferred_element_type=jnp.float32
    ) / TEMPERATURE
    own_row = lax.broadcasted_iota(jnp.int32, (SEGS, count), 0) + place * SEGS
    own_column = lax.broadcasted_iota(jnp.int32, (SEGS, count), 1)
    own_group = jnp.sum(jnp.where(own_row == own_column, groups[0:1], 0.0), axis=1, keepdims=True)
    own_same = (own_group == groups[0:1]) & (own_row != own_column)
    own_total = jnp.log(jnp.sum(jnp.where(own_same, jnp.exp(own_scores), 0.0), axis=1, keepdims=True))
    both = jnp.where(own_same, jnp.exp(own_scores - own_total) + jnp.exp(own_scores - column_total), 0.0)
    pulled = jnp.dot(both, embeddings, precision=HIGHEST, preferred_element_type=jnp.float32)
    for index in range(SEGS):
        where = positive[0, index]
        partner[index : index + 1, :] = gathered[where >> 4, pl.ds(where & (SEGS - 1), 1), :]
    factor = (count * 32) ** (-0.5) / TEMPERATURE
    embed_grad = factor * (pulled - 2.0 * partner[...])

    values = projected[...]
    inverse = lax.rsqrt(jnp.mean(values * values, axis=-1, keepdims=True) + EPS)
    outer = embed_grad * PROJ ** (-0.5)
    dotted = jnp.mean(values * outer, axis=-1, keepdims=True)
    projected_grad = inverse * outer - values * (inverse * inverse * inverse * dotted)
    derivative = lax.dot_general(
        pooled[...].astype(jnp.float32),
        projected_grad,
        (((0,), (0,)), ((), ())),
        precision=HIGHEST,
        preferred_element_type=jnp.float32,
    )
    hidden_grad = lax.dot_general(
        projected_grad, head[...].astype(jnp.float32), nt, precision=HIGHEST, preferred_element_type=jnp.float32
    ) * (1.0 / LEN)
    return derivative, hidden_grad


def weight_kernel(
    places, positive, gathered, projected, pooled, head, normed, slope, grad_out, keep_out, send_out,
    total, hidden_grad, derivative, partner,
):
    step = pl.program_id(0)

    @pl.when(step == 0)
    def _():
        derivative[...], hidden_grad[...] = loss_gradient(
            positive, gathered, projected, pooled, head, partner, places[0]
        )
        total[...] = jnp.zeros_like(total)

    shifted = []
    for index in range(STEP_SEGS):
        span = slice(index * LEN, (index + 1) * LEN)
        grad = (hidden_grad[pl.ds(step * STEP_SEGS + index, 1), :] * slope[span, :]).astype(jnp.bfloat16)
        grad_out[span, :] = grad
        shifted.append((later(grad), grad, earlier(grad)))
    rows = normed[...]
    for tap in range(TAPS):
        side = jnp.concatenate([parts[tap] for parts in shifted], axis=0)
        product = lax.dot_general(
            rows, side, (((0,), (0,)), ((), ())), preferred_element_type=jnp.float32
        )
        for block in range(C // 128):
            total[tap * (C // 128) + block] += product[:, block * 128 : (block + 1) * 128]

    @pl.when(step == STEPS - 1)
    def _():
        core = places[1]
        each = C // PLANE
        for target, which in ((keep_out, core), (send_out, 1 - core)):
            for chunk in range(PLANE):
                for block in range(HALF):
                    target[chunk, block * each : (block + 1) * each, :] = total[
                        which * HALF + block, chunk * each : (chunk + 1) * each, :
                    ]
                target[chunk, CONV_ROWS:, :] = derivative[
                    pl.ds(pl.multiple_of(which * (C // 2) + chunk * PROJ_ROWS, PROJ_ROWS), PROJ_ROWS), :
                ]


def weight_gradient(places, positive, gathered, projected, pooled, head, normed, slope):
    f32 = jnp.float32
    return pl.pallas_call(
        weight_kernel,
        grid=(STEPS,),
        in_specs=[
            whole((2,), SMEM),
            whole((1, SEGS), SMEM),
            whole((RANKS, SEGS + 8, PROJ)),
            whole((SEGS, PROJ)),
            whole((SEGS, C)),
            whole((C, PROJ)),
            pl.BlockSpec((ROWS, C), lambda i: (i, 0)),
            pl.BlockSpec((ROWS, C), lambda i: (i, 0)),
        ],
        out_specs=[
            pl.BlockSpec((ROWS, C), lambda i: (i, 0)),
            whole((PLANE, CHUNK, 128)),
            whole((PLANE, CHUNK, 128)),
        ],
        out_shape=[
            jax.ShapeDtypeStruct((SEGS * LEN, C), jnp.bfloat16),
            jax.ShapeDtypeStruct((PLANE, CHUNK, 128), f32),
            jax.ShapeDtypeStruct((PLANE, CHUNK, 128), f32),
        ],
        scratch_shapes=[
            VMEM((BLOCKS, C, 128), f32),
            VMEM((SEGS, C), f32),
            VMEM((C, PROJ), f32),
            VMEM((SEGS, PROJ), f32),
        ],
        compiler_params=pltpu.CompilerParams(vmem_limit_bytes=48 << 20),
        cost_estimate=pl.CostEstimate(flops=2 * SEGS * LEN * TAPS * C * C, bytes_accessed=12 << 20, transcendentals=1 << 16),
        name="weight_gradient",
    )(places, positive, gathered, projected, pooled, head, normed, slope)


def gain_kernel(grad, segments, weight, out, total):
    step = pl.program_id(0)

    @pl.when(step == 0)
    def _():
        total[...] = jnp.zeros_like(total)

    nt = (((1,), (1,)), ((), ()))
    for index in range(STEP_SEGS):
        middle = grad[index * LEN : (index + 1) * LEN, :]
        normed_grad = lax.dot_general(later(middle), weight[0], nt, preferred_element_type=jnp.float32)
        normed_grad += lax.dot_general(middle, weight[1], nt, preferred_element_type=jnp.float32)
        normed_grad += lax.dot_general(earlier(middle), weight[2], nt, preferred_element_type=jnp.float32)
        product = normed_grad * unit_rows(segments[0, index].astype(jnp.float32))
        total[...] += jnp.sum(product.reshape(LEN // 8, 8, C), axis=0)

    @pl.when(step == STEPS - 1)
    def _():
        summed = jnp.sum(total[...], axis=0, keepdims=True)
        for block in range(GAIN_ROWS):
            at = block % (C // 128)
            out[block : block + 1, :] = summed[:, at * 128 : (at + 1) * 128]


def gain_gradient(grad, segments, weight):
    f32 = jnp.float32
    return pl.pallas_call(
        gain_kernel,
        grid=(STEPS,),
        in_specs=[
            pl.BlockSpec((ROWS, C), lambda i: (i, 0)),
            pl.BlockSpec((1, STEP_SEGS, LEN, C), lambda i: (0, i, 0, 0)),
            whole((TAPS, C, C)),
        ],
        out_specs=whole((GAIN_ROWS, 128)),
        out_shape=jax.ShapeDtypeStruct((GAIN_ROWS, 128), f32),
        scratch_shapes=[VMEM((8, C), f32)],
        compiler_params=pltpu.CompilerParams(vmem_limit_bytes=48 << 20),
        cost_estimate=pl.CostEstimate(flops=2 * SEGS * LEN * TAPS * C * C, bytes_accessed=6 << 20, transcendentals=0),
        name="gain_gradient",
    )(grad, segments, weight)


def small_call(body, out_shape, name, *args):
    return pl.pallas_call(
        body,
        out_shape=out_shape,
        compiler_params=pltpu.CompilerParams(vmem_limit_bytes=24 << 20),
        cost_estimate=pl.CostEstimate(flops=1 << 20, bytes_accessed=4 << 20, transcendentals=0),
        name=name,
    )(*args)


def pair_sum_kernel(keep, received, gain, out):
    for chunk in range(PLANE):
        out[chunk, 0:CHUNK, :] = keep[chunk] + received[chunk]
        out[chunk, CHUNK:, :] = gain[...]


def plane_sum_kernel(received, out):
    summed = received[0]
    for source in range(1, PLANE):
        summed = summed + received[source]
    for depth in range(DEPTH):
        out[depth, 0:Z_CONV, :] = summed[depth * Z_CONV : (depth + 1) * Z_CONV, :]
        out[depth, Z_CONV : Z_CONV + Z_PROJ, :] = summed[
            CONV_ROWS + depth * Z_PROJ : CONV_ROWS + (depth + 1) * Z_PROJ, :
        ]
        out[depth, Z_CONV + Z_PROJ :, :] = summed[CHUNK : CHUNK + Z_CHUNK - Z_CONV - Z_PROJ, :]


def depth_sum_kernel(received, out, gain_out):
    summed = received[0]
    for source in range(1, DEPTH):
        summed = summed + received[source]
    for depth in range(DEPTH):
        out[depth] = summed
    gain_out[...] = summed[Z_CONV:, :]


def spread_kernel(received, out):
    for chunk in range(PLANE):
        for depth in range(DEPTH):
            out[chunk, depth * Z_CONV : (depth + 1) * Z_CONV, :] = received[depth, 0:Z_CONV, :]
            out[chunk, CONV_ROWS + depth * Z_PROJ : CONV_ROWS + (depth + 1) * Z_PROJ, :] = received[
                depth, Z_CONV : Z_CONV + Z_PROJ, :
            ]


def place_kernel(places, mine, other, gain_mine, gain_other, conv_out, gain_out, head_out):
    each = C // PLANE
    wide = C // 128
    first = places[1] == 0
    for chunk in range(PLANE):
        for half in range(2):
            rows = jnp.where(first == (half == 0), mine[chunk], other[chunk])
            for block in range(HALF):
                at = half * HALF + block
                conv_out[
                    at // wide, chunk * each : (chunk + 1) * each, (at % wide) * 128 : (at % wide + 1) * 128
                ] = rows[block * each : (block + 1) * each, :]
            start = half * (C // 2) + chunk * PROJ_ROWS
            head_out[start : start + PROJ_ROWS, :] = rows[CONV_ROWS:, :]
    summed = gain_mine[...] + gain_other[...]
    gain_out[...] = summed[Z_PROJ : Z_PROJ + wide, :]


def body(segments, conv_weight, gain, head, group, positive):
    f32 = jnp.float32
    plane = ("x", "yh", "yl")
    swap = [(0, 1), (1, 0)]
    places = jnp.stack([lax.axis_index(("x", "yh")), lax.axis_index("core")]).astype(jnp.int32)
    normed, slope, pooled, projected, send = forward(group, segments, conv_weight, gain.reshape(1, C), head)
    gathered = lax.all_to_all(send, ("x", "yh"), 0, 0)
    grad, keep, give = weight_gradient(places, positive, gathered, projected, pooled, head, normed, slope)
    received = lax.ppermute(give, "core", swap)
    gain_part = gain_gradient(grad, segments, conv_weight)
    paired = small_call(
        pair_sum_kernel, jax.ShapeDtypeStruct((PLANE, CHUNK + GAIN_ROWS, 128), f32), "pair_sum", keep, received, gain_part
    )
    across = lax.all_to_all(paired, plane, 0, 0)
    summed = small_call(plane_sum_kernel, jax.ShapeDtypeStruct((DEPTH, Z_CHUNK, 128), f32), "plane_sum", across)
    along = lax.all_to_all(summed, "z", 0, 0)
    done, gain_mine = small_call(
        depth_sum_kernel,
        (jax.ShapeDtypeStruct((DEPTH, Z_CHUNK, 128), f32), jax.ShapeDtypeStruct((8, 128), f32)),
        "depth_sum",
        along,
    )
    gain_other = lax.ppermute(gain_mine, "core", swap)
    back = lax.all_to_all(done, "z", 0, 0)
    spread = small_call(spread_kernel, jax.ShapeDtypeStruct((PLANE, CHUNK, 128), f32), "spread", back)
    mine = lax.all_to_all(spread, plane, 0, 0)
    other = lax.ppermute(mine, "core", swap)
    conv_grad, gain_grad, head_grad = pl.pallas_call(
        place_kernel,
        in_specs=[pl.BlockSpec(memory_space=SMEM)] + [pl.BlockSpec(memory_space=VMEM)] * 4,
        out_shape=(
            jax.ShapeDtypeStruct((TAPS, C, C), f32),
            jax.ShapeDtypeStruct((C // 128, 128), f32),
            jax.ShapeDtypeStruct((C, PROJ), f32),
        ),
        compiler_params=pltpu.CompilerParams(vmem_limit_bytes=24 << 20),
        name="place",
    )(places, mine, other, gain_mine, gain_other)
    return conv_grad, gain_grad.reshape(C), head_grad


def solution(mesh):
    fine = Mesh(mesh.devices.reshape(4, 2, 8, 2, 2), ("x", "yh", "z", "yl", "core"))
    row, grp = ("x", "yh"), ("z", "yl", "core")
    placed = (P(grp, row, None, None), P(), P(), P(), P(grp, row), P(grp, row))
    return jax.shard_map(body, mesh=fine, in_specs=placed, out_specs=(P(), P(), P()), check_vma=False)
```

```python
import functools

import jax
import jax.numpy as jnp
from jax import lax
from jax.experimental import pallas as pl
from jax.experimental.pallas import tpu as pltpu
from jax.sharding import Mesh, PartitionSpec as P

GAP = 2
TEMPERATURE = 0.1
EPS = 1e-05
HIGHEST = lax.Precision.HIGHEST

SEGS = 16
LEN = 128
C = 512
PROJ = 128
TAPS = 3
STEP_SEGS = 4
ROWS = STEP_SEGS * LEN
STEPS = SEGS // STEP_SEGS
JOIN = 2

RANKS = 8
PEERS = 32
STACKS = 4
BLOCKS = TAPS * C // 128
HALF = BLOCKS // 2
EACH = C // PEERS
CONV_ROWS = HALF * EACH
PROJ_ROWS = C // 2 // PEERS
CHUNK = CONV_ROWS + PROJ_ROWS
GAIN_ROWS = 8
LONG = CHUNK + GAIN_ROWS

VMEM = pltpu.VMEM
SMEM = pltpu.SMEM
DMA = pltpu.SemaphoreType.DMA
IN_HBM = pl.BlockSpec(memory_space=pl.ANY)
FULL = 67043328
IN_VMEM = pl.BlockSpec(memory_space=VMEM)
IN_SMEM = pl.BlockSpec(memory_space=SMEM)


def whole(shape, space=None):
    zeros = (0,) * len(shape)
    return pl.BlockSpec(shape, lambda *_: zeros, memory_space=space)


def later(rows):
    return jnp.concatenate([rows[GAP:], jnp.zeros((GAP, rows.shape[1]), rows.dtype)], axis=0)


def earlier(rows):
    return jnp.concatenate([jnp.zeros((GAP, rows.shape[1]), rows.dtype), rows[:-GAP]], axis=0)


def unit_rows(values):
    return values * lax.rsqrt(jnp.mean(values * values, axis=-1, keepdims=True) + EPS)


def forward_kernel(
    group_hbm, segments_hbm, weight_hbm, gain_hbm, head_hbm,
    normed_hbm, slope_hbm, pooled_out, projected_out, send_out,
    group, segments, weight, gain, head, pooled, normed_out, slope_out, step_sems, out_sems, sems,
):
    cubic = 0.044715
    scale = 0.7978845608028654

    def fetch(step):
        span = pl.ds(step * STEP_SEGS, STEP_SEGS)
        return pltpu.make_async_copy(segments_hbm.at[0, span], segments.at[span], step_sems.at[step])

    def store(step):
        span = pl.ds(step * STEP_SEGS, STEP_SEGS)
        return (
            pltpu.make_async_copy(normed_out.at[span], normed_hbm.at[span], out_sems.at[0, step]),
            pltpu.make_async_copy(slope_out.at[span], slope_hbm.at[span], out_sems.at[1, step]),
        )

    gain_copy = pltpu.make_async_copy(gain_hbm, gain, sems.at[0])
    weight_copy = pltpu.make_async_copy(weight_hbm, weight, sems.at[1])
    head_copy = pltpu.make_async_copy(head_hbm, head, sems.at[2])
    group_copy = pltpu.make_async_copy(group_hbm, group, sems.at[3])
    gain_copy.start()
    fetch(0).start()
    weight_copy.start()
    for step in range(1, STEPS):
        fetch(step).start()
    head_copy.start()
    group_copy.start()
    gain_copy.wait()

    def one_step(step, carry):
        fetch(step).wait()

        @pl.when(step == 0)
        def _():
            weight_copy.wait()

        for first in range(0, STEP_SEGS, JOIN):
            wide = []
            for index in range(first, first + JOIN):
                segment = step * STEP_SEGS + index
                normed = (unit_rows(segments[segment].astype(jnp.float32)) * gain[...]).astype(jnp.bfloat16)
                normed_out[segment] = normed
                wide.append(jnp.concatenate([earlier(normed), normed, later(normed)], axis=1))
            joined = jnp.dot(jnp.concatenate(wide, axis=0), weight[...], preferred_element_type=jnp.float32)
            for index in range(first, first + JOIN):
                segment = step * STEP_SEGS + index
                inputs = segments[segment].astype(jnp.float32)
                conv = joined[(index - first) * LEN : (index - first + 1) * LEN]
                square = conv * conv
                bent = jnp.tanh(conv * (scale + (scale * cubic) * square))
                half = 0.5 + 0.5 * bent
                hidden = inputs + conv * half
                slope_out[segment] = half + (0.5 * conv) * (1.0 - bent * bent) * (
                    scale + (3.0 * scale * cubic) * square
                )
                pooled[pl.ds(segment, 1), :] = jnp.sum(hidden, axis=0, keepdims=True) * (1.0 / LEN)
        for copy in store(step):
            copy.start()
        return carry

    lax.fori_loop(0, STEPS, one_step, 0)
    head_copy.wait()
    group_copy.wait()
    rounded = pooled[...].astype(jnp.bfloat16)
    pooled_out[...] = rounded
    projected = jnp.dot(rounded, head[...], preferred_element_type=jnp.float32)
    projected_out[...] = projected
    embedding = unit_rows(projected) * PROJ ** (-0.5)
    lane = lax.broadcasted_iota(jnp.int32, (8, 128), 1) & (SEGS - 1)
    groups = jnp.zeros((8, 128), jnp.int32)
    for index in range(SEGS):
        groups = jnp.where(lane == index, group[0, index], groups)
    groups = groups.astype(jnp.float32)
    for rank in range(RANKS):
        send_out[rank, 0:SEGS, :] = embedding
        send_out[rank, SEGS:, :] = groups
    for step in range(STEPS):
        for copy in store(step):
            copy.wait()


def forward(group, segments, weight, gain, head):
    f32 = jnp.float32
    bf16 = jnp.bfloat16
    return pl.pallas_call(
        forward_kernel,
        in_specs=[IN_HBM] * 5,
        out_specs=[IN_HBM] * 2 + [IN_VMEM] * 3,
        out_shape=[
            jax.ShapeDtypeStruct((SEGS, LEN, C), bf16),
            jax.ShapeDtypeStruct((SEGS, LEN, C), f32),
            jax.ShapeDtypeStruct((SEGS, C), bf16),
            jax.ShapeDtypeStruct((SEGS, PROJ), f32),
            jax.ShapeDtypeStruct((RANKS, SEGS + 8, PROJ), f32),
        ],
        scratch_shapes=[
            SMEM((1, SEGS), jnp.int32),
            VMEM((SEGS, LEN, C), bf16),
            VMEM((TAPS * C, C), bf16),
            VMEM((1, C), f32),
            VMEM((C, PROJ), bf16),
            VMEM((SEGS, C), f32),
            VMEM((SEGS, LEN, C), bf16),
            VMEM((SEGS, LEN, C), f32),
            DMA((STEPS,)),
            DMA((2, STEPS)),
            DMA((4,)),
        ],
        compiler_params=pltpu.CompilerParams(vmem_limit_bytes=FULL),
        cost_estimate=pl.CostEstimate(flops=2 * SEGS * LEN * TAPS * C * C, bytes_accessed=10 << 20, transcendentals=SEGS * LEN * C),
        name="forward",
    )(group, segments, weight.reshape(TAPS * C, C), gain, head)


def loss_gradient(positive, gathered, projected, pooled, head, partner, place):
    embeddings = gathered[:, 0:SEGS, :].reshape(RANKS * SEGS, PROJ)
    own = unit_rows(projected[...]) * PROJ ** (-0.5)
    count = RANKS * SEGS
    nt = (((1,), (1,)), ((), ()))
    lane = lax.broadcasted_iota(jnp.int32, (8, 128), 1)
    groups = jnp.zeros((8, 128), jnp.float32)
    for rank in range(RANKS):
        groups = jnp.where(lane >> 4 == rank, gathered[rank, SEGS:, :], groups)
    by_column = jnp.broadcast_to(groups[0:1], (count, count))
    by_row = by_column.T
    row = lax.broadcasted_iota(jnp.int32, (count, count), 0)
    column = lax.broadcasted_iota(jnp.int32, (count, count), 1)
    same = (by_row == by_column) & (row != column)
    scores = lax.dot_general(
        embeddings, embeddings, nt, precision=HIGHEST, preferred_element_type=jnp.float32
    ) / TEMPERATURE
    column_total = jnp.log(jnp.sum(jnp.where(same, jnp.exp(scores), 0.0), axis=0, keepdims=True))

    own_scores = lax.dot_general(
        own, embeddings, nt, precision=HIGHEST, preferred_element_type=jnp.float32
    ) / TEMPERATURE
    own_row = lax.broadcasted_iota(jnp.int32, (SEGS, count), 0) + place * SEGS
    own_column = lax.broadcasted_iota(jnp.int32, (SEGS, count), 1)
    own_group = jnp.sum(jnp.where(own_row == own_column, groups[0:1], 0.0), axis=1, keepdims=True)
    own_same = (own_group == groups[0:1]) & (own_row != own_column)
    own_total = jnp.log(jnp.sum(jnp.where(own_same, jnp.exp(own_scores), 0.0), axis=1, keepdims=True))
    both = jnp.where(own_same, jnp.exp(own_scores - own_total) + jnp.exp(own_scores - column_total), 0.0)
    pulled = jnp.dot(both, embeddings, precision=HIGHEST, preferred_element_type=jnp.float32)
    for index in range(SEGS):
        where = positive[0, index]
        partner[index : index + 1, :] = gathered[where >> 4, pl.ds(where & (SEGS - 1), 1), :]
    factor = (count * 32) ** (-0.5) / TEMPERATURE
    embed_grad = factor * (pulled - 2.0 * partner[...])

    values = projected[...]
    inverse = lax.rsqrt(jnp.mean(values * values, axis=-1, keepdims=True) + EPS)
    outer = embed_grad * PROJ ** (-0.5)
    dotted = jnp.mean(values * outer, axis=-1, keepdims=True)
    projected_grad = inverse * outer - values * (inverse * inverse * inverse * dotted)
    derivative = lax.dot_general(
        pooled[...].astype(jnp.float32),
        projected_grad,
        (((0,), (0,)), ((), ())),
        precision=HIGHEST,
        preferred_element_type=jnp.float32,
    )
    hidden_grad = lax.dot_general(
        projected_grad, head[...].astype(jnp.float32), nt, precision=HIGHEST, preferred_element_type=jnp.float32
    ) * (1.0 / LEN)
    return derivative, hidden_grad


def weight_kernel(
    places, positive_hbm, gathered, projected, pooled, head_hbm, normed_hbm, slope_hbm,
    grad_hbm, keep_out, send_out,
    total, hidden_grad, derivative, partner, positive, head, normed, slope, grad_out, sems, step_sems,
):
    def fetch(step):
        span = pl.ds(step * STEP_SEGS, STEP_SEGS)
        return (
            pltpu.make_async_copy(slope_hbm.at[span], slope.at[span], step_sems.at[0, step]),
            pltpu.make_async_copy(normed_hbm.at[span], normed.at[span], step_sems.at[1, step]),
        )

    def store(step):
        span = pl.ds(step * STEP_SEGS, STEP_SEGS)
        return pltpu.make_async_copy(grad_out.at[span], grad_hbm.at[span], step_sems.at[2, step])

    head_copy = pltpu.make_async_copy(head_hbm, head, sems.at[0])
    positive_copy = pltpu.make_async_copy(positive_hbm, positive, sems.at[1])
    head_copy.start()
    positive_copy.start()
    for step in range(STEPS):
        for copy in fetch(step):
            copy.start()
    head_copy.wait()
    positive_copy.wait()
    derivative[...], hidden_grad[...] = loss_gradient(
        positive, gathered, projected, pooled, head, partner, places[0]
    )
    total[...] = jnp.zeros_like(total)

    def one_step(step, carry):
        for copy in fetch(step):
            copy.wait()
        sides = []
        for index in range(STEP_SEGS):
            segment = step * STEP_SEGS + index
            grad = (hidden_grad[pl.ds(segment, 1), :] * slope[segment]).astype(jnp.bfloat16)
            grad_out[segment] = grad
            sides.append(jnp.concatenate([later(grad), grad, earlier(grad)], axis=1))
        rows = normed[pl.ds(step * STEP_SEGS, STEP_SEGS)].reshape(ROWS, C)
        product = lax.dot_general(
            rows, jnp.concatenate(sides, axis=0), (((0,), (0,)), ((), ())), preferred_element_type=jnp.float32
        )
        for block in range(BLOCKS):
            total[block] += product[:, block * 128 : (block + 1) * 128]
        store(step).start()
        return carry

    lax.fori_loop(0, STEPS, one_step, 0)
    core = places[1]
    for target, which in ((keep_out, core), (send_out, 1 - core)):
        for peer in range(PEERS):
            for block in range(HALF):
                target[peer, block * EACH : (block + 1) * EACH, :] = total[
                    which * HALF + block, peer * EACH : (peer + 1) * EACH, :
                ]
            target[peer, CONV_ROWS:, :] = derivative[
                pl.ds(pl.multiple_of(which * (C // 2) + peer * PROJ_ROWS, PROJ_ROWS), PROJ_ROWS), :
            ]
    for step in range(STEPS):
        store(step).wait()


def weight_gradient(places, positive, gathered, projected, pooled, head, normed, slope):
    f32 = jnp.float32
    bf16 = jnp.bfloat16
    return pl.pallas_call(
        weight_kernel,
        in_specs=[IN_SMEM, IN_HBM, IN_VMEM, IN_VMEM, IN_VMEM, IN_HBM, IN_HBM, IN_HBM],
        out_specs=[IN_HBM] + [IN_VMEM] * 2,
        out_shape=[
            jax.ShapeDtypeStruct((SEGS, LEN, C), bf16),
            jax.ShapeDtypeStruct((PEERS, CHUNK, 128), f32),
            jax.ShapeDtypeStruct((PEERS, CHUNK, 128), f32),
        ],
        scratch_shapes=[
            VMEM((BLOCKS, C, 128), f32),
            VMEM((SEGS, C), f32),
            VMEM((C, PROJ), f32),
            VMEM((SEGS, PROJ), f32),
            SMEM((1, SEGS), jnp.int32),
            VMEM((C, PROJ), bf16),
            VMEM((SEGS, LEN, C), bf16),
            VMEM((SEGS, LEN, C), f32),
            VMEM((SEGS, LEN, C), bf16),
            DMA((2,)),
            DMA((3, STEPS)),
        ],
        compiler_params=pltpu.CompilerParams(vmem_limit_bytes=FULL),
        cost_estimate=pl.CostEstimate(flops=2 * SEGS * LEN * TAPS * C * C, bytes_accessed=12 << 20, transcendentals=1 << 16),
        name="weight_gradient",
    )(places, positive, gathered, projected, pooled, head, normed, slope)


def gain_kernel(grad, segments, weight, out, total, wide):
    step = pl.program_id(0)

    @pl.when(step == 0)
    def _():
        total[...] = jnp.zeros_like(total)
        for tap in range(TAPS):
            wide[:, tap * C : (tap + 1) * C] = weight[tap]

    for first in range(0, STEP_SEGS, JOIN):
        sides = []
        for index in range(first, first + JOIN):
            middle = grad[index]
            sides.append(jnp.concatenate([later(middle), middle, earlier(middle)], axis=1))
        joined = lax.dot_general(
            jnp.concatenate(sides, axis=0), wide[...], (((1,), (1,)), ((), ())), preferred_element_type=jnp.float32
        )
        for index in range(first, first + JOIN):
            product = joined[(index - first) * LEN : (index - first + 1) * LEN] * unit_rows(
                segments[0, index].astype(jnp.float32)
            )
            total[...] += jnp.sum(product.reshape(LEN // 8, 8, C), axis=0)

    @pl.when(step == STEPS - 1)
    def _():
        summed = jnp.sum(total[...], axis=0, keepdims=True)
        for block in range(GAIN_ROWS):
            at = block % (C // 128)
            out[block : block + 1, :] = summed[:, at * 128 : (at + 1) * 128]


def gain_gradient(grad, segments, weight):
    f32 = jnp.float32
    return pl.pallas_call(
        gain_kernel,
        grid=(STEPS,),
        in_specs=[
            pl.BlockSpec((STEP_SEGS, LEN, C), lambda i: (i, 0, 0)),
            pl.BlockSpec((1, STEP_SEGS, LEN, C), lambda i: (0, i, 0, 0)),
            whole((TAPS, C, C)),
        ],
        out_specs=whole((GAIN_ROWS, 128)),
        out_shape=jax.ShapeDtypeStruct((GAIN_ROWS, 128), f32),
        scratch_shapes=[VMEM((8, C), f32), VMEM((C, TAPS * C), jnp.bfloat16)],
        compiler_params=pltpu.CompilerParams(vmem_limit_bytes=32 << 20),
        cost_estimate=pl.CostEstimate(flops=2 * SEGS * LEN * TAPS * C * C, bytes_accessed=6 << 20, transcendentals=0),
        name="gain_gradient",
    )(grad, segments, weight)


def small_call(body, out_shape, name, *args):
    return pl.pallas_call(
        body,
        out_shape=out_shape,
        compiler_params=pltpu.CompilerParams(vmem_limit_bytes=24 << 20),
        cost_estimate=pl.CostEstimate(flops=1 << 20, bytes_accessed=4 << 20, transcendentals=0),
        name=name,
    )(*args)


def peer_sum_kernel(received, gain, out):
    summed = received[0]
    for source in range(1, PEERS):
        summed = summed + received[source]
    for stack in range(STACKS):
        out[stack, 0:CHUNK, :] = summed
        out[stack, CHUNK:, :] = gain[...]


def stack_sum_kernel(received, out):
    summed = received[0]
    for source in range(1, STACKS):
        summed = summed + received[source]
    for peer in range(PEERS):
        out[peer] = summed


def place_kernel(flip, places, rows, *refs):
    gain_before = refs[0] if flip else None
    conv_hbm, head_hbm, gain_out, sems = refs[-4:]
    wide = C // 128
    half = 1 - places[1] if flip else places[1]
    copies = []
    for block in range(HALF):
        at = half * HALF + block
        tap = at >> 2
        lanes = pl.ds(pl.multiple_of((at & 3) * 128, 128), 128)
        source = rows.at[:, pl.ds(block * EACH, EACH), :]
        copies.append(pltpu.make_async_copy(source, conv_hbm.at[tap, :, :, lanes], sems.at[block]))
    source = rows.at[:, pl.ds(CONV_ROWS, PROJ_ROWS), :]
    copies.append(pltpu.make_async_copy(source, head_hbm.at[half], sems.at[HALF]))
    for copy in copies:
        copy.start()
    summed = rows[0, CHUNK:, :]
    for peer in range(1, PEERS):
        summed = summed + rows[peer, CHUNK:, :]
    if flip:
        gain_out[...] = (summed + gain_before[...])[0:wide, :]
    else:
        gain_out[...] = summed
    for copy in copies:
        copy.wait()


def place(flip, places, rows, before=None):
    f32 = jnp.float32
    return pl.pallas_call(
        functools.partial(place_kernel, flip),
        in_specs=[IN_SMEM, IN_VMEM] + ([IN_VMEM, IN_HBM, IN_HBM] if flip else []),
        out_specs=[IN_HBM, IN_HBM, IN_VMEM],
        out_shape=(
            jax.ShapeDtypeStruct((TAPS, PEERS, EACH, C), f32),
            jax.ShapeDtypeStruct((2, PEERS, PROJ_ROWS, PROJ), f32),
            jax.ShapeDtypeStruct((C // 128 if flip else GAIN_ROWS, 128), f32),
        ),
        scratch_shapes=[DMA((HALF + 1,))],
        input_output_aliases={3: 0, 4: 1} if flip else {},
        compiler_params=pltpu.CompilerParams(vmem_limit_bytes=24 << 20),
        cost_estimate=pl.CostEstimate(flops=1 << 20, bytes_accessed=4 << 20, transcendentals=0),
        name="place_other" if flip else "place_mine",
    )(places, rows, *((before[2], before[0], before[1]) if flip else ()))


def body(segments, conv_weight, gain, head, group, positive):
    f32 = jnp.float32
    peers = ("x", "yh", "zl", "yl")
    swap = [(0, 1), (1, 0)]
    places = jnp.stack([lax.axis_index(("x", "yh")), lax.axis_index("core")]).astype(jnp.int32)
    normed, slope, pooled, projected, send = forward(group, segments, conv_weight, gain.reshape(1, C), head)
    gathered = lax.all_to_all(send, ("x", "yh"), 0, 0)
    grad, keep, give = weight_gradient(places, positive, gathered, projected, pooled, head, normed, slope)
    received = lax.ppermute(give, "core", swap)
    paired = keep + received
    across = lax.all_to_all(paired, peers, 0, 0)
    gain_part = gain_gradient(grad, segments, conv_weight)
    summed = small_call(
        peer_sum_kernel, jax.ShapeDtypeStruct((STACKS, LONG, 128), f32), "peer_sum", across, gain_part
    )
    along = lax.all_to_all(summed, "zh", 0, 0)
    spread = small_call(stack_sum_kernel, jax.ShapeDtypeStruct((PEERS, LONG, 128), f32), "stack_sum", along)
    mine = lax.all_to_all(spread, peers, 0, 0)
    other = lax.ppermute(mine, "core", swap)
    conv_grad, head_grad, gain_grad = place(True, places, other, place(False, places, mine))
    return conv_grad.reshape(TAPS, C, C), gain_grad.reshape(C), head_grad.reshape(C, PROJ)


def solution(mesh):
    fine = Mesh(mesh.devices.reshape(4, 2, 4, 2, 2, 2), ("x", "yh", "zh", "zl", "yl", "core"))
    row, grp = ("x", "yh"), ("zh", "zl", "yl", "core")
    placed = (P(grp, row, None, None), P(), P(), P(), P(grp, row), P(grp, row))
    return jax.shard_map(body, mesh=fine, in_specs=placed, out_specs=(P(), P(), P()), check_vma=False)
```

```python
import functools

import jax
import jax.numpy as jnp
from jax import lax
from jax.experimental import pallas as pl
from jax.experimental.pallas import tpu as pltpu
from jax.sharding import Mesh, PartitionSpec as P

GAP = 2
TEMPERATURE = 0.1
EPS = 1e-05
HIGHEST = lax.Precision.HIGHEST

SEGS = 16
LEN = 128
C = 512
PROJ = 128
TAPS = 3
STEP_SEGS = 4
ROWS = STEP_SEGS * LEN
STEPS = SEGS // STEP_SEGS
JOIN = 2

RANKS = 8
PEERS = 32
STACKS = 4
BLOCKS = TAPS * C // 128
HALF = BLOCKS // 2
EACH = C // PEERS
CONV_ROWS = HALF * EACH
PROJ_ROWS = C // 2 // PEERS
CHUNK = CONV_ROWS + PROJ_ROWS
GAIN_ROWS = 8
LONG = CHUNK + GAIN_ROWS

PACK_POOLED = 2 * SEGS
PACK_HEAD = PACK_POOLED + SEGS * C // 128
PACK = PACK_HEAD + C

VMEM = pltpu.VMEM
SMEM = pltpu.SMEM
DMA = pltpu.SemaphoreType.DMA
IN_HBM = pl.BlockSpec(memory_space=pl.ANY)
FULL = 67043328
IN_VMEM = pl.BlockSpec(memory_space=VMEM)
IN_SMEM = pl.BlockSpec(memory_space=SMEM)


def whole(shape, space=None):
    zeros = (0,) * len(shape)
    return pl.BlockSpec(shape, lambda *_: zeros, memory_space=space)


def later(rows):
    return jnp.concatenate([rows[GAP:], jnp.zeros((GAP, rows.shape[1]), rows.dtype)], axis=0)


def earlier(rows):
    return jnp.concatenate([jnp.zeros((GAP, rows.shape[1]), rows.dtype), rows[:-GAP]], axis=0)


def unit_rows(values):
    return values * lax.rsqrt(jnp.mean(values * values, axis=-1, keepdims=True) + EPS)


def forward_kernel(
    group_hbm, positive_hbm, segments_hbm, weight_hbm, gain_hbm, head_hbm,
    normed_hbm, slope_hbm, pack_out, send_out,
    group, positive, segments, weight, gain, head, pooled, normed_out, slope_out, step_sems, out_sems, sems,
):
    cubic = 0.044715
    scale = 0.7978845608028654

    def fetch(step):
        span = pl.ds(step * STEP_SEGS, STEP_SEGS)
        return pltpu.make_async_copy(segments_hbm.at[0, span], segments.at[span], step_sems.at[step])

    def store(step):
        span = pl.ds(step * STEP_SEGS, STEP_SEGS)
        return (
            pltpu.make_async_copy(normed_out.at[span], normed_hbm.at[span], out_sems.at[0, step]),
            pltpu.make_async_copy(slope_out.at[span], slope_hbm.at[span], out_sems.at[1, step]),
        )

    gain_copy = pltpu.make_async_copy(gain_hbm, gain, sems.at[0])
    weight_copy = pltpu.make_async_copy(weight_hbm, weight, sems.at[1])
    head_copy = pltpu.make_async_copy(head_hbm, head, sems.at[2])
    group_copy = pltpu.make_async_copy(group_hbm, group, sems.at[3])
    positive_copy = pltpu.make_async_copy(positive_hbm, positive, sems.at[4])
    gain_copy.start()
    fetch(0).start()
    weight_copy.start()
    for step in range(1, STEPS):
        fetch(step).start()
    head_copy.start()
    group_copy.start()
    positive_copy.start()
    gain_copy.wait()

    def one_step(step, carry):
        fetch(step).wait()

        @pl.when(step == 0)
        def _():
            weight_copy.wait()

        for first in range(0, STEP_SEGS, JOIN):
            wide = []
            for index in range(first, first + JOIN):
                segment = step * STEP_SEGS + index
                normed = (unit_rows(segments[segment].astype(jnp.float32)) * gain[...]).astype(jnp.bfloat16)
                normed_out[segment] = normed
                wide.append(jnp.concatenate([earlier(normed), normed, later(normed)], axis=1))
            joined = jnp.dot(jnp.concatenate(wide, axis=0), weight[...], preferred_element_type=jnp.float32)
            for index in range(first, first + JOIN):
                segment = step * STEP_SEGS + index
                inputs = segments[segment].astype(jnp.float32)
                conv = joined[(index - first) * LEN : (index - first + 1) * LEN]
                square = conv * conv
                bent = jnp.tanh(conv * (scale + (scale * cubic) * square))
                half = 0.5 + 0.5 * bent
                hidden = inputs + conv * half
                slope_out[segment] = half + (0.5 * conv) * (1.0 - bent * bent) * (
                    scale + (3.0 * scale * cubic) * square
                )
                pooled[pl.ds(segment, 1), :] = jnp.sum(hidden, axis=0, keepdims=True) * (1.0 / LEN)
        for copy in store(step):
            copy.start()
        return carry

    lax.fori_loop(0, STEPS, one_step, 0)
    head_copy.wait()
    group_copy.wait()
    positive_copy.wait()
    rounded = pooled[...].astype(jnp.bfloat16)
    projected = jnp.dot(rounded, head[...], preferred_element_type=jnp.float32)
    pack_out[0:SEGS, :] = projected
    for index in range(SEGS):
        row = jnp.full((1, PROJ), positive[0, index], jnp.int32)
        pack_out[SEGS + index : SEGS + index + 1, :] = row.astype(jnp.float32)
    for block in range(C // 128):
        at = PACK_POOLED + block * SEGS
        pack_out[at : at + SEGS, :] = rounded[:, block * 128 : (block + 1) * 128].astype(jnp.float32)
    pack_out[PACK_HEAD:, :] = head[...].astype(jnp.float32)
    embedding = unit_rows(projected) * PROJ ** (-0.5)
    lane = lax.broadcasted_iota(jnp.int32, (8, 128), 1) & (SEGS - 1)
    groups = jnp.zeros((8, 128), jnp.int32)
    for index in range(SEGS):
        groups = jnp.where(lane == index, group[0, index], groups)
    groups = groups.astype(jnp.float32)
    for rank in range(RANKS):
        send_out[rank, 0:SEGS, :] = embedding
        send_out[rank, SEGS:, :] = groups
    for step in range(STEPS):
        for copy in store(step):
            copy.wait()


def forward(group, positive, segments, weight, gain, head):
    f32 = jnp.float32
    bf16 = jnp.bfloat16
    return pl.pallas_call(
        forward_kernel,
        in_specs=[IN_HBM] * 6,
        out_specs=[IN_HBM] * 2 + [IN_VMEM] * 2,
        out_shape=[
            jax.ShapeDtypeStruct((SEGS, LEN, C), bf16),
            jax.ShapeDtypeStruct((SEGS, LEN, C), f32),
            jax.ShapeDtypeStruct((PACK, PROJ), f32),
            jax.ShapeDtypeStruct((RANKS, SEGS + 8, PROJ), f32),
        ],
        scratch_shapes=[
            SMEM((1, SEGS), jnp.int32),
            SMEM((1, SEGS), jnp.int32),
            VMEM((SEGS, LEN, C), bf16),
            VMEM((TAPS * C, C), bf16),
            VMEM((1, C), f32),
            VMEM((C, PROJ), bf16),
            VMEM((SEGS, C), f32),
            VMEM((SEGS, LEN, C), bf16),
            VMEM((SEGS, LEN, C), f32),
            DMA((STEPS,)),
            DMA((2, STEPS)),
            DMA((5,)),
        ],
        compiler_params=pltpu.CompilerParams(vmem_limit_bytes=FULL),
        cost_estimate=pl.CostEstimate(flops=2 * SEGS * LEN * TAPS * C * C, bytes_accessed=10 << 20, transcendentals=SEGS * LEN * C),
        name="forward",
    )(group, positive, segments, weight.reshape(TAPS * C, C), gain, head)


def loss_gradient(gathered, pack, place):
    projected = pack[0:SEGS, :]
    pooled = jnp.concatenate(
        [pack[PACK_POOLED + block * SEGS : PACK_POOLED + (block + 1) * SEGS, :] for block in range(C // 128)], axis=1
    )
    embeddings = gathered[:, 0:SEGS, :].reshape(RANKS * SEGS, PROJ)
    own = unit_rows(projected) * PROJ ** (-0.5)
    count = RANKS * SEGS
    nt = (((1,), (1,)), ((), ()))
    lane = lax.broadcasted_iota(jnp.int32, (8, 128), 1)
    groups = jnp.zeros((8, 128), jnp.float32)
    for rank in range(RANKS):
        groups = jnp.where(lane >> 4 == rank, gathered[rank, SEGS:, :], groups)
    by_column = jnp.broadcast_to(groups[0:1], (count, count))
    by_row = by_column.T
    row = lax.broadcasted_iota(jnp.int32, (count, count), 0)
    column = lax.broadcasted_iota(jnp.int32, (count, count), 1)
    same = (by_row == by_column) & (row != column)
    scores = lax.dot_general(
        embeddings, embeddings, nt, precision=HIGHEST, preferred_element_type=jnp.float32
    ) / TEMPERATURE
    column_total = jnp.log(jnp.sum(jnp.where(same, jnp.exp(scores), 0.0), axis=0, keepdims=True))

    own_scores = lax.dot_general(
        own, embeddings, nt, precision=HIGHEST, preferred_element_type=jnp.float32
    ) / TEMPERATURE
    own_row = lax.broadcasted_iota(jnp.int32, (SEGS, count), 0) + place * SEGS
    own_column = lax.broadcasted_iota(jnp.int32, (SEGS, count), 1)
    own_group = jnp.sum(jnp.where(own_row == own_column, groups[0:1], 0.0), axis=1, keepdims=True)
    own_same = (own_group == groups[0:1]) & (own_row != own_column)
    own_total = jnp.log(jnp.sum(jnp.where(own_same, jnp.exp(own_scores), 0.0), axis=1, keepdims=True))
    both = jnp.where(own_same, jnp.exp(own_scores - own_total) + jnp.exp(own_scores - column_total), 0.0)
    pulled = jnp.dot(both, embeddings, precision=HIGHEST, preferred_element_type=jnp.float32)
    picked = (pack[SEGS : 2 * SEGS, :] == own_column.astype(jnp.float32)).astype(jnp.float32)
    partner = jnp.dot(picked, embeddings, precision=HIGHEST, preferred_element_type=jnp.float32)
    factor = (count * 32) ** (-0.5) / TEMPERATURE
    embed_grad = factor * (pulled - 2.0 * partner)

    values = projected
    inverse = lax.rsqrt(jnp.mean(values * values, axis=-1, keepdims=True) + EPS)
    outer = embed_grad * PROJ ** (-0.5)
    dotted = jnp.mean(values * outer, axis=-1, keepdims=True)
    projected_grad = inverse * outer - values * (inverse * inverse * inverse * dotted)
    derivative = lax.dot_general(
        pooled,
        projected_grad,
        (((0,), (0,)), ((), ())),
        precision=HIGHEST,
        preferred_element_type=jnp.float32,
    )
    hidden_grad = lax.dot_general(
        projected_grad, pack[PACK_HEAD:, :], nt, precision=HIGHEST, preferred_element_type=jnp.float32
    ) * (1.0 / LEN)
    return derivative, hidden_grad


def weight_kernel(
    places, gathered, pack, normed_hbm, slope_hbm,
    grad_hbm, keep_out, send_out,
    total, hidden_grad, derivative, normed, slope, grad_out, step_sems,
):
    def fetch(step):
        span = pl.ds(step * STEP_SEGS, STEP_SEGS)
        return (
            pltpu.make_async_copy(slope_hbm.at[span], slope.at[span], step_sems.at[0, step]),
            pltpu.make_async_copy(normed_hbm.at[span], normed.at[span], step_sems.at[1, step]),
        )

    def store(step):
        span = pl.ds(step * STEP_SEGS, STEP_SEGS)
        return pltpu.make_async_copy(grad_out.at[span], grad_hbm.at[span], step_sems.at[2, step])

    for step in range(STEPS):
        for copy in fetch(step):
            copy.start()
    derivative[...], hidden_grad[...] = loss_gradient(gathered, pack, places[0])
    total[...] = jnp.zeros_like(total)

    def one_step(step, carry):
        for copy in fetch(step):
            copy.wait()
        sides = []
        for index in range(STEP_SEGS):
            segment = step * STEP_SEGS + index
            grad = (hidden_grad[pl.ds(segment, 1), :] * slope[segment]).astype(jnp.bfloat16)
            grad_out[segment] = grad
            sides.append(jnp.concatenate([later(grad), grad, earlier(grad)], axis=1))
        rows = normed[pl.ds(step * STEP_SEGS, STEP_SEGS)].reshape(ROWS, C)
        product = lax.dot_general(
            rows, jnp.concatenate(sides, axis=0), (((0,), (0,)), ((), ())), preferred_element_type=jnp.float32
        )
        for block in range(BLOCKS):
            total[block] += product[:, block * 128 : (block + 1) * 128]
        store(step).start()
        return carry

    lax.fori_loop(0, STEPS, one_step, 0)
    core = places[1]
    for target, which in ((keep_out, core), (send_out, 1 - core)):
        for peer in range(PEERS):
            for block in range(HALF):
                target[peer, block * EACH : (block + 1) * EACH, :] = total[
                    which * HALF + block, peer * EACH : (peer + 1) * EACH, :
                ]
            target[peer, CONV_ROWS:, :] = derivative[
                pl.ds(pl.multiple_of(which * (C // 2) + peer * PROJ_ROWS, PROJ_ROWS), PROJ_ROWS), :
            ]
    for step in range(STEPS):
        store(step).wait()


def weight_gradient(places, gathered, pack, normed, slope):
    f32 = jnp.float32
    bf16 = jnp.bfloat16
    return pl.pallas_call(
        weight_kernel,
        in_specs=[IN_SMEM, IN_VMEM, IN_VMEM, IN_HBM, IN_HBM],
        out_specs=[IN_HBM] + [IN_VMEM] * 2,
        out_shape=[
            jax.ShapeDtypeStruct((SEGS, LEN, C), bf16),
            jax.ShapeDtypeStruct((PEERS, CHUNK, 128), f32),
            jax.ShapeDtypeStruct((PEERS, CHUNK, 128), f32),
        ],
        scratch_shapes=[
            VMEM((BLOCKS, C, 128), f32),
            VMEM((SEGS, C), f32),
            VMEM((C, PROJ), f32),
            VMEM((SEGS, LEN, C), bf16),
            VMEM((SEGS, LEN, C), f32),
            VMEM((SEGS, LEN, C), bf16),
            DMA((3, STEPS)),
        ],
        compiler_params=pltpu.CompilerParams(vmem_limit_bytes=48 << 20),
        cost_estimate=pl.CostEstimate(flops=2 * SEGS * LEN * TAPS * C * C, bytes_accessed=12 << 20, transcendentals=1 << 16),
        name="weight_gradient",
    )(places, gathered, pack, normed, slope)


def gain_kernel(grad, segments, weight, out, total, wide):
    step = pl.program_id(0)

    @pl.when(step == 0)
    def _():
        total[...] = jnp.zeros_like(total)
        for tap in range(TAPS):
            wide[:, tap * C : (tap + 1) * C] = weight[tap]

    for first in range(0, STEP_SEGS, JOIN):
        sides = []
        for index in range(first, first + JOIN):
            middle = grad[index]
            sides.append(jnp.concatenate([later(middle), middle, earlier(middle)], axis=1))
        joined = lax.dot_general(
            jnp.concatenate(sides, axis=0), wide[...], (((1,), (1,)), ((), ())), preferred_element_type=jnp.float32
        )
        for index in range(first, first + JOIN):
            product = joined[(index - first) * LEN : (index - first + 1) * LEN] * unit_rows(
                segments[0, index].astype(jnp.float32)
            )
            total[...] += jnp.sum(product.reshape(LEN // 8, 8, C), axis=0)

    @pl.when(step == STEPS - 1)
    def _():
        summed = jnp.sum(total[...], axis=0, keepdims=True)
        for block in range(GAIN_ROWS):
            at = block % (C // 128)
            out[block : block + 1, :] = summed[:, at * 128 : (at + 1) * 128]


def gain_gradient(grad, segments, weight):
    f32 = jnp.float32
    return pl.pallas_call(
        gain_kernel,
        grid=(STEPS,),
        in_specs=[
            pl.BlockSpec((STEP_SEGS, LEN, C), lambda i: (i, 0, 0)),
            pl.BlockSpec((1, STEP_SEGS, LEN, C), lambda i: (0, i, 0, 0)),
            whole((TAPS, C, C)),
        ],
        out_specs=whole((GAIN_ROWS, 128)),
        out_shape=jax.ShapeDtypeStruct((GAIN_ROWS, 128), f32),
        scratch_shapes=[VMEM((8, C), f32), VMEM((C, TAPS * C), jnp.bfloat16)],
        compiler_params=pltpu.CompilerParams(vmem_limit_bytes=32 << 20),
        cost_estimate=pl.CostEstimate(flops=2 * SEGS * LEN * TAPS * C * C, bytes_accessed=6 << 20, transcendentals=0),
        name="gain_gradient",
    )(grad, segments, weight)


def small_call(body, out_shape, name, *args):
    return pl.pallas_call(
        body,
        out_shape=out_shape,
        compiler_params=pltpu.CompilerParams(vmem_limit_bytes=24 << 20),
        cost_estimate=pl.CostEstimate(flops=1 << 20, bytes_accessed=4 << 20, transcendentals=0),
        name=name,
    )(*args)


def pair_sum_kernel(keep, received, gain, out, gain_out):
    gain_out[...] = gain[...]
    for peer in range(PEERS):
        out[peer] = keep[peer] + received[peer]


def peer_sum_kernel(received, gain, out):
    summed = received[0]
    for source in range(1, PEERS):
        summed = summed + received[source]
    for stack in range(STACKS):
        out[stack, 0:CHUNK, :] = summed
        out[stack, CHUNK:, :] = gain[...]


def stack_sum_kernel(received, out):
    summed = received[0]
    for source in range(1, STACKS):
        summed = summed + received[source]
    for peer in range(PEERS):
        out[peer] = summed


def place_kernel(flip, places, rows, *refs):
    gain_before = refs[0] if flip else None
    conv_hbm, head_hbm, gain_out, sems = refs[-4:]
    wide = C // 128
    half = 1 - places[1] if flip else places[1]
    copies = []
    for block in range(HALF):
        at = half * HALF + block
        tap = at >> 2
        lanes = pl.ds(pl.multiple_of((at & 3) * 128, 128), 128)
        source = rows.at[:, pl.ds(block * EACH, EACH), :]
        copies.append(pltpu.make_async_copy(source, conv_hbm.at[tap, :, :, lanes], sems.at[block]))
    source = rows.at[:, pl.ds(CONV_ROWS, PROJ_ROWS), :]
    copies.append(pltpu.make_async_copy(source, head_hbm.at[half], sems.at[HALF]))
    for copy in copies:
        copy.start()
    summed = rows[0, CHUNK:, :]
    for peer in range(1, PEERS):
        summed = summed + rows[peer, CHUNK:, :]
    if flip:
        gain_out[...] = (summed + gain_before[...])[0:wide, :]
    else:
        gain_out[...] = summed
    for copy in copies:
        copy.wait()


def place(flip, places, rows, before=None):
    f32 = jnp.float32
    return pl.pallas_call(
        functools.partial(place_kernel, flip),
        in_specs=[IN_SMEM, IN_VMEM] + ([IN_VMEM, IN_HBM, IN_HBM] if flip else []),
        out_specs=[IN_HBM, IN_HBM, IN_VMEM],
        out_shape=(
            jax.ShapeDtypeStruct((TAPS, PEERS, EACH, C), f32),
            jax.ShapeDtypeStruct((2, PEERS, PROJ_ROWS, PROJ), f32),
            jax.ShapeDtypeStruct((C // 128 if flip else GAIN_ROWS, 128), f32),
        ),
        scratch_shapes=[DMA((HALF + 1,))],
        input_output_aliases={3: 0, 4: 1} if flip else {},
        compiler_params=pltpu.CompilerParams(vmem_limit_bytes=24 << 20),
        cost_estimate=pl.CostEstimate(flops=1 << 20, bytes_accessed=4 << 20, transcendentals=0),
        name="place_other" if flip else "place_mine",
    )(places, rows, *((before[2], before[0], before[1]) if flip else ()))


def body(segments, conv_weight, gain, head, group, positive):
    f32 = jnp.float32
    peers = ("x", "yh", "zl", "yl")
    swap = [(0, 1), (1, 0)]
    places = jnp.stack([lax.axis_index(("x", "yh")), lax.axis_index("core")]).astype(jnp.int32)
    normed, slope, pack, send = forward(group, positive, segments, conv_weight, gain.reshape(1, C), head)
    gathered = lax.all_to_all(send, ("x", "yh"), 0, 0)
    grad, keep, give = weight_gradient(places, gathered, pack, normed, slope)
    received = lax.ppermute(give, "core", swap)
    gain_part = gain_gradient(grad, segments, conv_weight)
    paired, gain_part = small_call(
        pair_sum_kernel,
        (jax.ShapeDtypeStruct((PEERS, CHUNK, 128), f32), jax.ShapeDtypeStruct((GAIN_ROWS, 128), f32)),
        "pair_sum",
        keep,
        received,
        gain_part,
    )
    across = lax.all_to_all(paired, peers, 0, 0)
    summed = small_call(
        peer_sum_kernel, jax.ShapeDtypeStruct((STACKS, LONG, 128), f32), "peer_sum", across, gain_part
    )
    along = lax.all_to_all(summed, "zh", 0, 0)
    spread = small_call(stack_sum_kernel, jax.ShapeDtypeStruct((PEERS, LONG, 128), f32), "stack_sum", along)
    mine = lax.all_to_all(spread, peers, 0, 0)
    other = lax.ppermute(mine, "core", swap)
    conv_grad, head_grad, gain_grad = place(True, places, other, place(False, places, mine))
    return conv_grad.reshape(TAPS, C, C), gain_grad.reshape(C), head_grad.reshape(C, PROJ)


def solution(mesh):
    fine = Mesh(mesh.devices.reshape(4, 2, 4, 2, 2, 2), ("x", "yh", "zh", "zl", "yl", "core"))
    row, grp = ("x", "yh"), ("zh", "zl", "yl", "core")
    placed = (P(grp, row, None, None), P(), P(), P(), P(grp, row), P(grp, row))
    return jax.shard_map(body, mesh=fine, in_specs=placed, out_specs=(P(), P(), P()), check_vma=False)
```

```python
import functools

import jax
import jax.numpy as jnp
from jax import lax
from jax.experimental import pallas as pl
from jax.experimental.pallas import tpu as pltpu
from jax.sharding import Mesh, PartitionSpec as P

GAP = 2
TEMPERATURE = 0.1
EPS = 1e-05
HIGHEST = lax.Precision.HIGHEST

SEGS = 16
LEN = 128
C = 512
PROJ = 128
TAPS = 3
STEP_SEGS = 8
F_STEP = 4
F_STEPS = SEGS // F_STEP
F_JOIN = 4
ROWS = STEP_SEGS * LEN
STEPS = SEGS // STEP_SEGS
JOIN = 2

RANKS = 8
PEERS = 32
STACKS = 4
BLOCKS = TAPS * C // 128
HALF = BLOCKS // 2
EACH = C // PEERS
CONV_ROWS = HALF * EACH
PROJ_ROWS = C // 2 // PEERS
CHUNK = CONV_ROWS + PROJ_ROWS
GAIN_ROWS = 8
LONG = CHUNK + GAIN_ROWS

PACK_POOLED = 2 * SEGS
PACK_HEAD = PACK_POOLED + SEGS * C // 128
PACK = PACK_HEAD + C

VMEM = pltpu.VMEM
SMEM = pltpu.SMEM
DMA = pltpu.SemaphoreType.DMA
IN_HBM = pl.BlockSpec(memory_space=pl.ANY)
FULL = 67043328
IN_VMEM = pl.BlockSpec(memory_space=VMEM)
IN_SMEM = pl.BlockSpec(memory_space=SMEM)


def whole(shape, space=None):
    zeros = (0,) * len(shape)
    return pl.BlockSpec(shape, lambda *_: zeros, memory_space=space)


def later(rows):
    return jnp.concatenate([rows[GAP:], jnp.zeros((GAP, rows.shape[1]), rows.dtype)], axis=0)


def earlier(rows):
    return jnp.concatenate([jnp.zeros((GAP, rows.shape[1]), rows.dtype), rows[:-GAP]], axis=0)


def unit_rows(values):
    return values * lax.rsqrt(jnp.mean(values * values, axis=-1, keepdims=True) + EPS)


def forward_kernel(
    group_hbm, positive_hbm, segments_hbm, weight_hbm, gain_hbm, head_hbm,
    normed_hbm, slope_hbm, pack_out, send_out,
    group, positive, segments, weight, gain, head, pooled, normed_out, slope_out, step_sems, out_sems, sems,
):
    cubic = 0.044715
    scale = 0.7978845608028654

    def fetch(step):
        span = pl.ds(step * F_STEP, F_STEP)
        return pltpu.make_async_copy(segments_hbm.at[0, span], segments.at[span], step_sems.at[step])

    def store(step):
        span = pl.ds(step * F_STEP, F_STEP)
        return (
            pltpu.make_async_copy(normed_out.at[span], normed_hbm.at[span], out_sems.at[0, step]),
            pltpu.make_async_copy(slope_out.at[span], slope_hbm.at[span], out_sems.at[1, step]),
        )

    gain_copy = pltpu.make_async_copy(gain_hbm, gain, sems.at[0])
    weight_copy = pltpu.make_async_copy(weight_hbm, weight, sems.at[1])
    head_copy = pltpu.make_async_copy(head_hbm, head, sems.at[2])
    group_copy = pltpu.make_async_copy(group_hbm, group, sems.at[3])
    positive_copy = pltpu.make_async_copy(positive_hbm, positive, sems.at[4])
    gain_copy.start()
    fetch(0).start()
    weight_copy.start()
    for step in range(1, F_STEPS):
        fetch(step).start()
    head_copy.start()
    group_copy.start()
    positive_copy.start()
    gain_copy.wait()

    def one_step(step, carry):
        fetch(step).wait()

        @pl.when(step == 0)
        def _():
            weight_copy.wait()

        for first in range(0, F_STEP, F_JOIN):
            wide = []
            for index in range(first, first + F_JOIN):
                segment = step * F_STEP + index
                normed = (unit_rows(segments[segment].astype(jnp.float32)) * gain[...]).astype(jnp.bfloat16)
                normed_out[segment] = normed
                wide.append(jnp.concatenate([earlier(normed), normed, later(normed)], axis=1))
            joined = jnp.dot(jnp.concatenate(wide, axis=0), weight[...], preferred_element_type=jnp.float32)
            for index in range(first, first + F_JOIN):
                segment = step * F_STEP + index
                inputs = segments[segment].astype(jnp.float32)
                conv = joined[(index - first) * LEN : (index - first + 1) * LEN]
                square = conv * conv
                bent = jnp.tanh(conv * (scale + (scale * cubic) * square))
                half = 0.5 + 0.5 * bent
                hidden = inputs + conv * half
                slope_out[segment] = half + (0.5 * conv) * (1.0 - bent * bent) * (
                    scale + (3.0 * scale * cubic) * square
                )
                pooled[pl.ds(segment, 1), :] = jnp.sum(hidden, axis=0, keepdims=True) * (1.0 / LEN)
        for copy in store(step):
            copy.start()
        return carry

    lax.fori_loop(0, F_STEPS, one_step, 0)
    head_copy.wait()
    group_copy.wait()
    positive_copy.wait()
    rounded = pooled[...].astype(jnp.bfloat16)
    projected = jnp.dot(rounded, head[...], preferred_element_type=jnp.float32)
    pack_out[0:SEGS, :] = projected
    for index in range(SEGS):
        row = jnp.full((1, PROJ), positive[0, index], jnp.int32)
        pack_out[SEGS + index : SEGS + index + 1, :] = row.astype(jnp.float32)
    for block in range(C // 128):
        at = PACK_POOLED + block * SEGS
        pack_out[at : at + SEGS, :] = rounded[:, block * 128 : (block + 1) * 128].astype(jnp.float32)
    pack_out[PACK_HEAD:, :] = head[...].astype(jnp.float32)
    embedding = unit_rows(projected) * PROJ ** (-0.5)
    lane = lax.broadcasted_iota(jnp.int32, (8, 128), 1) & (SEGS - 1)
    groups = jnp.zeros((8, 128), jnp.int32)
    for index in range(SEGS):
        groups = jnp.where(lane == index, group[0, index], groups)
    groups = groups.astype(jnp.float32)
    for rank in range(RANKS):
        send_out[rank, 0:SEGS, :] = embedding
        send_out[rank, SEGS:, :] = groups
    for step in range(F_STEPS):
        for copy in store(step):
            copy.wait()


def forward(group, positive, segments, weight, gain, head):
    f32 = jnp.float32
    bf16 = jnp.bfloat16
    return pl.pallas_call(
        forward_kernel,
        in_specs=[IN_HBM] * 6,
        out_specs=[IN_HBM] * 2 + [IN_VMEM] * 2,
        out_shape=[
            jax.ShapeDtypeStruct((SEGS, LEN, C), bf16),
            jax.ShapeDtypeStruct((SEGS, LEN, C), f32),
            jax.ShapeDtypeStruct((PACK, PROJ), f32),
            jax.ShapeDtypeStruct((RANKS, SEGS + 8, PROJ), f32),
        ],
        scratch_shapes=[
            SMEM((1, SEGS), jnp.int32),
            SMEM((1, SEGS), jnp.int32),
            VMEM((SEGS, LEN, C), bf16),
            VMEM((TAPS * C, C), bf16),
            VMEM((1, C), f32),
            VMEM((C, PROJ), bf16),
            VMEM((SEGS, C), f32),
            VMEM((SEGS, LEN, C), bf16),
            VMEM((SEGS, LEN, C), f32),
            DMA((F_STEPS,)),
            DMA((2, F_STEPS)),
            DMA((5,)),
        ],
        compiler_params=pltpu.CompilerParams(vmem_limit_bytes=FULL),
        cost_estimate=pl.CostEstimate(flops=2 * SEGS * LEN * TAPS * C * C, bytes_accessed=10 << 20, transcendentals=SEGS * LEN * C),
        name="forward",
    )(group, positive, segments, weight.reshape(TAPS * C, C), gain, head)


def loss_gradient(gathered, pack, place):
    projected = pack[0:SEGS, :]
    pooled = jnp.concatenate(
        [pack[PACK_POOLED + block * SEGS : PACK_POOLED + (block + 1) * SEGS, :] for block in range(C // 128)], axis=1
    )
    embeddings = gathered[:, 0:SEGS, :].reshape(RANKS * SEGS, PROJ)
    own = unit_rows(projected) * PROJ ** (-0.5)
    count = RANKS * SEGS
    nt = (((1,), (1,)), ((), ()))
    lane = lax.broadcasted_iota(jnp.int32, (8, 128), 1)
    groups = jnp.zeros((8, 128), jnp.float32)
    for rank in range(RANKS):
        groups = jnp.where(lane >> 4 == rank, gathered[rank, SEGS:, :], groups)
    by_column = jnp.broadcast_to(groups[0:1], (count, count))
    by_row = by_column.T
    row = lax.broadcasted_iota(jnp.int32, (count, count), 0)
    column = lax.broadcasted_iota(jnp.int32, (count, count), 1)
    same = (by_row == by_column) & (row != column)
    scores = lax.dot_general(
        embeddings, embeddings, nt, precision=HIGHEST, preferred_element_type=jnp.float32
    ) / TEMPERATURE
    column_total = jnp.log(jnp.sum(jnp.where(same, jnp.exp(scores), 0.0), axis=0, keepdims=True))

    own_scores = lax.dot_general(
        own, embeddings, nt, precision=HIGHEST, preferred_element_type=jnp.float32
    ) / TEMPERATURE
    own_row = lax.broadcasted_iota(jnp.int32, (SEGS, count), 0) + place * SEGS
    own_column = lax.broadcasted_iota(jnp.int32, (SEGS, count), 1)
    own_group = jnp.sum(jnp.where(own_row == own_column, groups[0:1], 0.0), axis=1, keepdims=True)
    own_same = (own_group == groups[0:1]) & (own_row != own_column)
    own_total = jnp.log(jnp.sum(jnp.where(own_same, jnp.exp(own_scores), 0.0), axis=1, keepdims=True))
    both = jnp.where(own_same, jnp.exp(own_scores - own_total) + jnp.exp(own_scores - column_total), 0.0)
    pulled = jnp.dot(both, embeddings, precision=HIGHEST, preferred_element_type=jnp.float32)
    picked = (pack[SEGS : 2 * SEGS, :] == own_column.astype(jnp.float32)).astype(jnp.float32)
    partner = jnp.dot(picked, embeddings, precision=HIGHEST, preferred_element_type=jnp.float32)
    factor = (count * 32) ** (-0.5) / TEMPERATURE
    embed_grad = factor * (pulled - 2.0 * partner)

    values = projected
    inverse = lax.rsqrt(jnp.mean(values * values, axis=-1, keepdims=True) + EPS)
    outer = embed_grad * PROJ ** (-0.5)
    dotted = jnp.mean(values * outer, axis=-1, keepdims=True)
    projected_grad = inverse * outer - values * (inverse * inverse * inverse * dotted)
    derivative = lax.dot_general(
        pooled,
        projected_grad,
        (((0,), (0,)), ((), ())),
        precision=HIGHEST,
        preferred_element_type=jnp.float32,
    )
    hidden_grad = lax.dot_general(
        projected_grad, pack[PACK_HEAD:, :], nt, precision=HIGHEST, preferred_element_type=jnp.float32
    ) * (1.0 / LEN)
    return derivative, hidden_grad


def weight_kernel(
    places, gathered, pack, normed_hbm, slope_hbm,
    grad_hbm, keep_out, send_out,
    total, hidden_grad, derivative, normed, slope, grad_out, step_sems,
):
    def fetch(step):
        span = pl.ds(step * STEP_SEGS, STEP_SEGS)
        return (
            pltpu.make_async_copy(slope_hbm.at[span], slope.at[span], step_sems.at[0, step]),
            pltpu.make_async_copy(normed_hbm.at[span], normed.at[span], step_sems.at[1, step]),
        )

    def store(step):
        span = pl.ds(step * STEP_SEGS, STEP_SEGS)
        return pltpu.make_async_copy(grad_out.at[span], grad_hbm.at[span], step_sems.at[2, step])

    for step in range(STEPS):
        for copy in fetch(step):
            copy.start()
    derivative[...], hidden_grad[...] = loss_gradient(gathered, pack, places[0])
    total[...] = jnp.zeros_like(total)

    def one_step(step, carry):
        for copy in fetch(step):
            copy.wait()
        sides = []
        for index in range(STEP_SEGS):
            segment = step * STEP_SEGS + index
            grad = (hidden_grad[pl.ds(segment, 1), :] * slope[segment]).astype(jnp.bfloat16)
            grad_out[segment] = grad
            sides.append(jnp.concatenate([later(grad), grad, earlier(grad)], axis=1))
        rows = normed[pl.ds(step * STEP_SEGS, STEP_SEGS)].reshape(ROWS, C)
        product = lax.dot_general(
            rows, jnp.concatenate(sides, axis=0), (((0,), (0,)), ((), ())), preferred_element_type=jnp.float32
        )
        for block in range(BLOCKS):
            total[block] += product[:, block * 128 : (block + 1) * 128]
        store(step).start()
        return carry

    lax.fori_loop(0, STEPS, one_step, 0)
    core = places[1]
    for target, which in ((keep_out, core), (send_out, 1 - core)):
        for peer in range(PEERS):
            for block in range(HALF):
                target[peer, block * EACH : (block + 1) * EACH, :] = total[
                    which * HALF + block, peer * EACH : (peer + 1) * EACH, :
                ]
            target[peer, CONV_ROWS:, :] = derivative[
                pl.ds(pl.multiple_of(which * (C // 2) + peer * PROJ_ROWS, PROJ_ROWS), PROJ_ROWS), :
            ]
    for step in range(STEPS):
        store(step).wait()


def weight_gradient(places, gathered, pack, normed, slope):
    f32 = jnp.float32
    bf16 = jnp.bfloat16
    return pl.pallas_call(
        weight_kernel,
        in_specs=[IN_SMEM, IN_VMEM, IN_VMEM, IN_HBM, IN_HBM],
        out_specs=[IN_HBM] + [IN_VMEM] * 2,
        out_shape=[
            jax.ShapeDtypeStruct((SEGS, LEN, C), bf16),
            jax.ShapeDtypeStruct((PEERS, CHUNK, 128), f32),
            jax.ShapeDtypeStruct((PEERS, CHUNK, 128), f32),
        ],
        scratch_shapes=[
            VMEM((BLOCKS, C, 128), f32),
            VMEM((SEGS, C), f32),
            VMEM((C, PROJ), f32),
            VMEM((SEGS, LEN, C), bf16),
            VMEM((SEGS, LEN, C), f32),
            VMEM((SEGS, LEN, C), bf16),
            DMA((3, STEPS)),
        ],
        compiler_params=pltpu.CompilerParams(vmem_limit_bytes=48 << 20),
        cost_estimate=pl.CostEstimate(flops=2 * SEGS * LEN * TAPS * C * C, bytes_accessed=12 << 20, transcendentals=1 << 16),
        name="weight_gradient",
    )(places, gathered, pack, normed, slope)


def gain_kernel(grad, segments, weight, out, total, wide):
    step = pl.program_id(0)

    @pl.when(step == 0)
    def _():
        total[...] = jnp.zeros_like(total)
        for tap in range(TAPS):
            wide[:, tap * C : (tap + 1) * C] = weight[tap]

    for first in range(0, STEP_SEGS, JOIN):
        sides = []
        for index in range(first, first + JOIN):
            middle = grad[index]
            sides.append(jnp.concatenate([later(middle), middle, earlier(middle)], axis=1))
        joined = lax.dot_general(
            jnp.concatenate(sides, axis=0), wide[...], (((1,), (1,)), ((), ())), preferred_element_type=jnp.float32
        )
        for index in range(first, first + JOIN):
            product = joined[(index - first) * LEN : (index - first + 1) * LEN] * unit_rows(
                segments[0, index].astype(jnp.float32)
            )
            total[...] += jnp.sum(product.reshape(LEN // 8, 8, C), axis=0)

    @pl.when(step == STEPS - 1)
    def _():
        summed = jnp.sum(total[...], axis=0, keepdims=True)
        for block in range(GAIN_ROWS):
            at = block % (C // 128)
            out[block : block + 1, :] = summed[:, at * 128 : (at + 1) * 128]


def gain_gradient(grad, segments, weight):
    f32 = jnp.float32
    return pl.pallas_call(
        gain_kernel,
        grid=(STEPS,),
        in_specs=[
            pl.BlockSpec((STEP_SEGS, LEN, C), lambda i: (i, 0, 0)),
            pl.BlockSpec((1, STEP_SEGS, LEN, C), lambda i: (0, i, 0, 0)),
            whole((TAPS, C, C)),
        ],
        out_specs=whole((GAIN_ROWS, 128)),
        out_shape=jax.ShapeDtypeStruct((GAIN_ROWS, 128), f32),
        scratch_shapes=[VMEM((8, C), f32), VMEM((C, TAPS * C), jnp.bfloat16)],
        compiler_params=pltpu.CompilerParams(vmem_limit_bytes=32 << 20),
        cost_estimate=pl.CostEstimate(flops=2 * SEGS * LEN * TAPS * C * C, bytes_accessed=6 << 20, transcendentals=0),
        name="gain_gradient",
    )(grad, segments, weight)


def small_call(body, out_shape, name, *args):
    return pl.pallas_call(
        body,
        out_shape=out_shape,
        compiler_params=pltpu.CompilerParams(vmem_limit_bytes=24 << 20),
        cost_estimate=pl.CostEstimate(flops=1 << 20, bytes_accessed=4 << 20, transcendentals=0),
        name=name,
    )(*args)


def pair_sum_kernel(keep, received, gain, out, gain_out):
    gain_out[...] = gain[...]
    for peer in range(PEERS):
        out[peer] = keep[peer] + received[peer]


def peer_sum_kernel(received, gain, out):
    summed = received[0]
    for source in range(1, PEERS):
        summed = summed + received[source]
    out[0:CHUNK, :] = summed
    out[CHUNK:, :] = gain[...]


def stack_sum_kernel(own, after, across, before, out):
    summed = (own[...] + across[...]) + (after[...] + before[...])
    for peer in range(PEERS):
        out[peer] = summed


def place_kernel(flip, places, rows, *refs):
    gain_before = refs[0] if flip else None
    conv_hbm, head_hbm, gain_out, sems = refs[-4:]
    wide = C // 128
    half = 1 - places[1] if flip else places[1]
    copies = []
    for block in range(HALF):
        at = half * HALF + block
        tap = at >> 2
        lanes = pl.ds(pl.multiple_of((at & 3) * 128, 128), 128)
        source = rows.at[:, pl.ds(block * EACH, EACH), :]
        copies.append(pltpu.make_async_copy(source, conv_hbm.at[tap, :, :, lanes], sems.at[block]))
    source = rows.at[:, pl.ds(CONV_ROWS, PROJ_ROWS), :]
    copies.append(pltpu.make_async_copy(source, head_hbm.at[half], sems.at[HALF]))
    for copy in copies:
        copy.start()
    summed = rows[0, CHUNK:, :]
    for peer in range(1, PEERS):
        summed = summed + rows[peer, CHUNK:, :]
    if flip:
        gain_out[...] = (summed + gain_before[...])[0:wide, :]
    else:
        gain_out[...] = summed
    for copy in copies:
        copy.wait()


def place(flip, places, rows, before=None):
    f32 = jnp.float32
    return pl.pallas_call(
        functools.partial(place_kernel, flip),
        in_specs=[IN_SMEM, IN_VMEM] + ([IN_VMEM, IN_HBM, IN_HBM] if flip else []),
        out_specs=[IN_HBM, IN_HBM, IN_VMEM],
        out_shape=(
            jax.ShapeDtypeStruct((TAPS, PEERS, EACH, C), f32),
            jax.ShapeDtypeStruct((2, PEERS, PROJ_ROWS, PROJ), f32),
            jax.ShapeDtypeStruct((C // 128 if flip else GAIN_ROWS, 128), f32),
        ),
        scratch_shapes=[DMA((HALF + 1,))],
        input_output_aliases={3: 0, 4: 1} if flip else {},
        compiler_params=pltpu.CompilerParams(vmem_limit_bytes=24 << 20),
        cost_estimate=pl.CostEstimate(flops=1 << 20, bytes_accessed=4 << 20, transcendentals=0),
        name="place_other" if flip else "place_mine",
    )(places, rows, *((before[2], before[0], before[1]) if flip else ()))


def body(segments, conv_weight, gain, head, group, positive):
    f32 = jnp.float32
    peers = ("x", "yh", "zl", "yl")
    swap = [(0, 1), (1, 0)]
    places = jnp.stack([lax.axis_index(("x", "yh")), lax.axis_index("core")]).astype(jnp.int32)
    normed, slope, pack, send = forward(group, positive, segments, conv_weight, gain.reshape(1, C), head)
    gathered = lax.all_to_all(send, ("x", "yh"), 0, 0)
    grad, keep, give = weight_gradient(places, gathered, pack, normed, slope)
    received = lax.ppermute(give, "core", swap)
    gain_part = gain_gradient(grad, segments, conv_weight)
    paired, gain_part = small_call(
        pair_sum_kernel,
        (jax.ShapeDtypeStruct((PEERS, CHUNK, 128), f32), jax.ShapeDtypeStruct((GAIN_ROWS, 128), f32)),
        "pair_sum",
        keep,
        received,
        gain_part,
    )
    across = lax.all_to_all(paired, peers, 0, 0)
    chunk = small_call(peer_sum_kernel, jax.ShapeDtypeStruct((LONG, 128), f32), "peer_sum", across, gain_part)
    rings = [lax.ppermute(chunk, "zh", [(i, (i + d) % STACKS) for i in range(STACKS)]) for d in (1, 2, 3)]
    spread = small_call(
        stack_sum_kernel, jax.ShapeDtypeStruct((PEERS, LONG, 128), f32), "stack_sum", chunk, *rings
    )
    mine = lax.all_to_all(spread, peers, 0, 0)
    other = lax.ppermute(mine, "core", swap)
    conv_grad, head_grad, gain_grad = place(True, places, other, place(False, places, mine))
    return conv_grad.reshape(TAPS, C, C), gain_grad.reshape(C), head_grad.reshape(C, PROJ)


def solution(mesh):
    fine = Mesh(mesh.devices.reshape(4, 2, 4, 2, 2, 2), ("x", "yh", "zh", "zl", "yl", "core"))
    row, grp = ("x", "yh"), ("zh", "zl", "yl", "core")
    placed = (P(grp, row, None, None), P(), P(), P(), P(grp, row), P(grp, row))
    return jax.shard_map(body, mesh=fine, in_specs=placed, out_specs=(P(), P(), P()), check_vma=False)
```

```python
import functools

import jax
import jax.numpy as jnp
from jax import lax
from jax.experimental import pallas as pl
from jax.experimental.pallas import tpu as pltpu
from jax.sharding import Mesh, PartitionSpec as P

GAP = 2
TEMPERATURE = 0.1
EPS = 1e-05
HIGHEST = lax.Precision.HIGHEST

SEGS = 16
LEN = 128
C = 512
PROJ = 128
TAPS = 3
STEP_SEGS = 8
F_STEP = 4
F_STEPS = SEGS // F_STEP
F_JOIN = 4
ROWS = STEP_SEGS * LEN
STEPS = SEGS // STEP_SEGS
JOIN = 2

RANKS = 8
PEERS = 32
STACKS = 4
BLOCKS = TAPS * C // 128
HALF = BLOCKS // 2
EACH = C // PEERS
CONV_ROWS = HALF * EACH
PROJ_ROWS = C // 2 // PEERS
CHUNK = CONV_ROWS + PROJ_ROWS
GAIN_ROWS = 8
LONG = CHUNK + GAIN_ROWS

PACK_POOLED = 2 * SEGS
PACK_HEAD = PACK_POOLED + SEGS * C // 128
PACK = PACK_HEAD + C

VMEM = pltpu.VMEM
SMEM = pltpu.SMEM
DMA = pltpu.SemaphoreType.DMA
IN_HBM = pl.BlockSpec(memory_space=pl.ANY)
FULL = 67043328
IN_VMEM = pl.BlockSpec(memory_space=VMEM)
IN_SMEM = pl.BlockSpec(memory_space=SMEM)


def whole(shape, space=None):
    zeros = (0,) * len(shape)
    return pl.BlockSpec(shape, lambda *_: zeros, memory_space=space)


def later(rows):
    return jnp.concatenate([rows[GAP:], jnp.zeros((GAP, rows.shape[1]), rows.dtype)], axis=0)


def earlier(rows):
    return jnp.concatenate([jnp.zeros((GAP, rows.shape[1]), rows.dtype), rows[:-GAP]], axis=0)


def unit_rows(values):
    return values * lax.rsqrt(jnp.mean(values * values, axis=-1, keepdims=True) + EPS)


def forward_kernel(
    group_hbm, positive_hbm, segments_hbm, weight_hbm, gain_hbm, head_hbm,
    normed_hbm, slope_hbm, pack_hbm, send_hbm,
    group, positive, segments, weight, gain, head, pooled, normed_out, slope_out, pack_out, send_out,
    step_sems, out_sems, sems,
):
    cubic = 0.044715
    scale = 0.7978845608028654

    def fetch(step):
        span = pl.ds(step * F_STEP, F_STEP)
        return pltpu.make_async_copy(segments_hbm.at[0, span], segments.at[span], step_sems.at[step])

    def store(step):
        span = pl.ds(step * F_STEP, F_STEP)
        return (
            pltpu.make_async_copy(normed_out.at[span], normed_hbm.at[span], out_sems.at[0, step]),
            pltpu.make_async_copy(slope_out.at[span], slope_hbm.at[span], out_sems.at[1, step]),
        )

    gain_copy = pltpu.make_async_copy(gain_hbm, gain, sems.at[0])
    weight_copy = pltpu.make_async_copy(weight_hbm, weight, sems.at[1])
    head_copy = pltpu.make_async_copy(head_hbm, head, sems.at[2])
    group_copy = pltpu.make_async_copy(group_hbm, group, sems.at[3])
    positive_copy = pltpu.make_async_copy(positive_hbm, positive, sems.at[4])
    start_rows, head_rows = pl.ds(0, PACK_HEAD), pl.ds(PACK_HEAD, C)
    head_store = pltpu.make_async_copy(pack_out.at[head_rows], pack_hbm.at[head_rows], sems.at[5])
    pack_store = pltpu.make_async_copy(pack_out.at[start_rows], pack_hbm.at[start_rows], sems.at[6])
    send_store = pltpu.make_async_copy(send_out, send_hbm, sems.at[7])
    gain_copy.start()
    fetch(0).start()
    weight_copy.start()
    for step in range(1, F_STEPS):
        fetch(step).start()
    head_copy.start()
    group_copy.start()
    positive_copy.start()
    gain_copy.wait()

    def one_step(step, carry):
        fetch(step).wait()

        @pl.when(step == 0)
        def _():
            weight_copy.wait()

        for first in range(0, F_STEP, F_JOIN):
            wide = []
            for index in range(first, first + F_JOIN):
                segment = step * F_STEP + index
                normed = (unit_rows(segments[segment].astype(jnp.float32)) * gain[...]).astype(jnp.bfloat16)
                normed_out[segment] = normed
                wide.append(jnp.concatenate([earlier(normed), normed, later(normed)], axis=1))
            joined = jnp.dot(jnp.concatenate(wide, axis=0), weight[...], preferred_element_type=jnp.float32)
            for index in range(first, first + F_JOIN):
                segment = step * F_STEP + index
                inputs = segments[segment].astype(jnp.float32)
                conv = joined[(index - first) * LEN : (index - first + 1) * LEN]
                square = conv * conv
                bent = jnp.tanh(conv * (scale + (scale * cubic) * square))
                half = 0.5 + 0.5 * bent
                hidden = inputs + conv * half
                slope_out[segment] = half + (0.5 * conv) * (1.0 - bent * bent) * (
                    scale + (3.0 * scale * cubic) * square
                )
                pooled[pl.ds(segment, 1), :] = jnp.sum(hidden, axis=0, keepdims=True) * (1.0 / LEN)
        for copy in store(step):
            copy.start()
        return carry

    lax.fori_loop(0, F_STEPS, one_step, 0)
    head_copy.wait()
    pack_out[PACK_HEAD:, :] = head[...].astype(jnp.float32)
    head_store.start()
    group_copy.wait()
    positive_copy.wait()
    rounded = pooled[...].astype(jnp.bfloat16)
    projected = jnp.dot(rounded, head[...], preferred_element_type=jnp.float32)
    pack_out[0:SEGS, :] = projected
    for index in range(SEGS):
        row = jnp.full((1, PROJ), positive[0, index], jnp.int32)
        pack_out[SEGS + index : SEGS + index + 1, :] = row.astype(jnp.float32)
    for block in range(C // 128):
        at = PACK_POOLED + block * SEGS
        pack_out[at : at + SEGS, :] = rounded[:, block * 128 : (block + 1) * 128].astype(jnp.float32)
    embedding = unit_rows(projected) * PROJ ** (-0.5)
    lane = lax.broadcasted_iota(jnp.int32, (8, 128), 1) & (SEGS - 1)
    groups = jnp.zeros((8, 128), jnp.int32)
    for index in range(SEGS):
        groups = jnp.where(lane == index, group[0, index], groups)
    groups = groups.astype(jnp.float32)
    for rank in range(RANKS):
        send_out[rank, 0:SEGS, :] = embedding
        send_out[rank, SEGS:, :] = groups
    send_store.start()
    pack_store.start()
    head_store.wait()
    send_store.wait()
    pack_store.wait()
    for step in range(F_STEPS):
        for copy in store(step):
            copy.wait()


def forward(group, positive, segments, weight, gain, head):
    f32 = jnp.float32
    bf16 = jnp.bfloat16
    return pl.pallas_call(
        forward_kernel,
        in_specs=[IN_HBM] * 6,
        out_specs=[IN_HBM] * 4,
        out_shape=[
            jax.ShapeDtypeStruct((SEGS, LEN, C), bf16),
            jax.ShapeDtypeStruct((SEGS, LEN, C), f32),
            jax.ShapeDtypeStruct((PACK, PROJ), f32),
            jax.ShapeDtypeStruct((RANKS, SEGS + 8, PROJ), f32),
        ],
        scratch_shapes=[
            SMEM((1, SEGS), jnp.int32),
            SMEM((1, SEGS), jnp.int32),
            VMEM((SEGS, LEN, C), bf16),
            VMEM((TAPS * C, C), bf16),
            VMEM((1, C), f32),
            VMEM((C, PROJ), bf16),
            VMEM((SEGS, C), f32),
            VMEM((SEGS, LEN, C), bf16),
            VMEM((SEGS, LEN, C), f32),
            VMEM((PACK, PROJ), f32),
            VMEM((RANKS, SEGS + 8, PROJ), f32),
            DMA((F_STEPS,)),
            DMA((2, F_STEPS)),
            DMA((8,)),
        ],
        compiler_params=pltpu.CompilerParams(vmem_limit_bytes=FULL),
        cost_estimate=pl.CostEstimate(flops=2 * SEGS * LEN * TAPS * C * C, bytes_accessed=10 << 20, transcendentals=SEGS * LEN * C),
        name="forward",
    )(group, positive, segments, weight.reshape(TAPS * C, C), gain, head)


def loss_gradient(gathered, pack, place):
    projected = pack[0:SEGS, :]
    pooled = jnp.concatenate(
        [pack[PACK_POOLED + block * SEGS : PACK_POOLED + (block + 1) * SEGS, :] for block in range(C // 128)], axis=1
    )
    embeddings = gathered[:, 0:SEGS, :].reshape(RANKS * SEGS, PROJ)
    own = unit_rows(projected) * PROJ ** (-0.5)
    count = RANKS * SEGS
    nt = (((1,), (1,)), ((), ()))
    lane = lax.broadcasted_iota(jnp.int32, (8, 128), 1)
    groups = jnp.zeros((8, 128), jnp.float32)
    for rank in range(RANKS):
        groups = jnp.where(lane >> 4 == rank, gathered[rank, SEGS:, :], groups)
    by_column = jnp.broadcast_to(groups[0:1], (count, count))
    by_row = by_column.T
    row = lax.broadcasted_iota(jnp.int32, (count, count), 0)
    column = lax.broadcasted_iota(jnp.int32, (count, count), 1)
    same = (by_row == by_column) & (row != column)
    scores = lax.dot_general(
        embeddings, embeddings, nt, precision=HIGHEST, preferred_element_type=jnp.float32
    ) / TEMPERATURE
    column_total = jnp.log(jnp.sum(jnp.where(same, jnp.exp(scores), 0.0), axis=0, keepdims=True))

    own_scores = lax.dot_general(
        own, embeddings, nt, precision=HIGHEST, preferred_element_type=jnp.float32
    ) / TEMPERATURE
    own_row = lax.broadcasted_iota(jnp.int32, (SEGS, count), 0) + place * SEGS
    own_column = lax.broadcasted_iota(jnp.int32, (SEGS, count), 1)
    own_group = jnp.sum(jnp.where(own_row == own_column, groups[0:1], 0.0), axis=1, keepdims=True)
    own_same = (own_group == groups[0:1]) & (own_row != own_column)
    own_total = jnp.log(jnp.sum(jnp.where(own_same, jnp.exp(own_scores), 0.0), axis=1, keepdims=True))
    both = jnp.where(own_same, jnp.exp(own_scores - own_total) + jnp.exp(own_scores - column_total), 0.0)
    pulled = jnp.dot(both, embeddings, precision=HIGHEST, preferred_element_type=jnp.float32)
    picked = (pack[SEGS : 2 * SEGS, :] == own_column.astype(jnp.float32)).astype(jnp.float32)
    partner = jnp.dot(picked, embeddings, precision=HIGHEST, preferred_element_type=jnp.float32)
    factor = (count * 32) ** (-0.5) / TEMPERATURE
    embed_grad = factor * (pulled - 2.0 * partner)

    values = projected
    inverse = lax.rsqrt(jnp.mean(values * values, axis=-1, keepdims=True) + EPS)
    outer = embed_grad * PROJ ** (-0.5)
    dotted = jnp.mean(values * outer, axis=-1, keepdims=True)
    projected_grad = inverse * outer - values * (inverse * inverse * inverse * dotted)
    derivative = lax.dot_general(
        pooled,
        projected_grad,
        (((0,), (0,)), ((), ())),
        precision=HIGHEST,
        preferred_element_type=jnp.float32,
    )
    hidden_grad = lax.dot_general(
        projected_grad, pack[PACK_HEAD:, :], nt, precision=HIGHEST, preferred_element_type=jnp.float32
    ) * (1.0 / LEN)
    return derivative, hidden_grad


def weight_kernel(
    places, gathered, pack, normed_hbm, slope_hbm,
    grad_hbm, keep_out, send_out,
    total, hidden_grad, derivative, normed, slope, grad_out, step_sems,
):
    def fetch(step):
        span = pl.ds(step * STEP_SEGS, STEP_SEGS)
        return (
            pltpu.make_async_copy(slope_hbm.at[span], slope.at[span], step_sems.at[0, step]),
            pltpu.make_async_copy(normed_hbm.at[span], normed.at[span], step_sems.at[1, step]),
        )

    def store(step):
        span = pl.ds(step * STEP_SEGS, STEP_SEGS)
        return pltpu.make_async_copy(grad_out.at[span], grad_hbm.at[span], step_sems.at[2, step])

    for step in range(STEPS):
        for copy in fetch(step):
            copy.start()
    derivative[...], hidden_grad[...] = loss_gradient(gathered, pack, places[0])
    total[...] = jnp.zeros_like(total)

    def one_step(step, carry):
        for copy in fetch(step):
            copy.wait()
        sides = []
        for index in range(STEP_SEGS):
            segment = step * STEP_SEGS + index
            grad = (hidden_grad[pl.ds(segment, 1), :] * slope[segment]).astype(jnp.bfloat16)
            grad_out[segment] = grad
            sides.append(jnp.concatenate([later(grad), grad, earlier(grad)], axis=1))
        rows = normed[pl.ds(step * STEP_SEGS, STEP_SEGS)].reshape(ROWS, C)
        product = lax.dot_general(
            rows, jnp.concatenate(sides, axis=0), (((0,), (0,)), ((), ())), preferred_element_type=jnp.float32
        )
        for block in range(BLOCKS):
            total[block] += product[:, block * 128 : (block + 1) * 128]
        store(step).start()
        return carry

    lax.fori_loop(0, STEPS, one_step, 0)
    core = places[1]
    for target, which in ((keep_out, core), (send_out, 1 - core)):
        for peer in range(PEERS):
            for block in range(HALF):
                target[peer, block * EACH : (block + 1) * EACH, :] = total[
                    which * HALF + block, peer * EACH : (peer + 1) * EACH, :
                ]
            target[peer, CONV_ROWS:, :] = derivative[
                pl.ds(pl.multiple_of(which * (C // 2) + peer * PROJ_ROWS, PROJ_ROWS), PROJ_ROWS), :
            ]
    for step in range(STEPS):
        store(step).wait()


def weight_gradient(places, gathered, pack, normed, slope):
    f32 = jnp.float32
    bf16 = jnp.bfloat16
    return pl.pallas_call(
        weight_kernel,
        in_specs=[IN_SMEM, IN_VMEM, IN_VMEM, IN_HBM, IN_HBM],
        out_specs=[IN_HBM] + [IN_VMEM] * 2,
        out_shape=[
            jax.ShapeDtypeStruct((SEGS, LEN, C), bf16),
            jax.ShapeDtypeStruct((PEERS, CHUNK, 128), f32),
            jax.ShapeDtypeStruct((PEERS, CHUNK, 128), f32),
        ],
        scratch_shapes=[
            VMEM((BLOCKS, C, 128), f32),
            VMEM((SEGS, C), f32),
            VMEM((C, PROJ), f32),
            VMEM((SEGS, LEN, C), bf16),
            VMEM((SEGS, LEN, C), f32),
            VMEM((SEGS, LEN, C), bf16),
            DMA((3, STEPS)),
        ],
        compiler_params=pltpu.CompilerParams(vmem_limit_bytes=48 << 20),
        cost_estimate=pl.CostEstimate(flops=2 * SEGS * LEN * TAPS * C * C, bytes_accessed=12 << 20, transcendentals=1 << 16),
        name="weight_gradient",
    )(places, gathered, pack, normed, slope)


def gain_kernel(grad, segments, weight, out, total, wide):
    step = pl.program_id(0)

    @pl.when(step == 0)
    def _():
        total[...] = jnp.zeros_like(total)
        for tap in range(TAPS):
            wide[:, tap * C : (tap + 1) * C] = weight[tap]

    for first in range(0, STEP_SEGS, JOIN):
        sides = []
        for index in range(first, first + JOIN):
            middle = grad[index]
            sides.append(jnp.concatenate([later(middle), middle, earlier(middle)], axis=1))
        joined = lax.dot_general(
            jnp.concatenate(sides, axis=0), wide[...], (((1,), (1,)), ((), ())), preferred_element_type=jnp.float32
        )
        for index in range(first, first + JOIN):
            product = joined[(index - first) * LEN : (index - first + 1) * LEN] * unit_rows(
                segments[0, index].astype(jnp.float32)
            )
            total[...] += jnp.sum(product.reshape(LEN // 8, 8, C), axis=0)

    @pl.when(step == STEPS - 1)
    def _():
        summed = jnp.sum(total[...], axis=0, keepdims=True)
        for block in range(GAIN_ROWS):
            at = block % (C // 128)
            out[block : block + 1, :] = summed[:, at * 128 : (at + 1) * 128]


def gain_gradient(grad, segments, weight):
    f32 = jnp.float32
    return pl.pallas_call(
        gain_kernel,
        grid=(STEPS,),
        in_specs=[
            pl.BlockSpec((STEP_SEGS, LEN, C), lambda i: (i, 0, 0)),
            pl.BlockSpec((1, STEP_SEGS, LEN, C), lambda i: (0, i, 0, 0)),
            whole((TAPS, C, C)),
        ],
        out_specs=whole((GAIN_ROWS, 128)),
        out_shape=jax.ShapeDtypeStruct((GAIN_ROWS, 128), f32),
        scratch_shapes=[VMEM((8, C), f32), VMEM((C, TAPS * C), jnp.bfloat16)],
        compiler_params=pltpu.CompilerParams(vmem_limit_bytes=32 << 20),
        cost_estimate=pl.CostEstimate(flops=2 * SEGS * LEN * TAPS * C * C, bytes_accessed=6 << 20, transcendentals=0),
        name="gain_gradient",
    )(grad, segments, weight)


def small_call(body, out_shape, name, *args):
    return pl.pallas_call(
        body,
        out_shape=out_shape,
        compiler_params=pltpu.CompilerParams(vmem_limit_bytes=24 << 20),
        cost_estimate=pl.CostEstimate(flops=1 << 20, bytes_accessed=4 << 20, transcendentals=0),
        name=name,
    )(*args)


def pair_sum_kernel(keep, received, gain, out, gain_out):
    gain_out[...] = gain[...]
    for peer in range(PEERS):
        out[peer] = keep[peer] + received[peer]


def peer_sum_kernel(received, gain, out):
    summed = received[0]
    for source in range(1, PEERS):
        summed = summed + received[source]
    out[0:CHUNK, :] = summed
    out[CHUNK:, :] = gain[...]


def stack_sum_kernel(own, after, across, before, out):
    summed = (own[...] + across[...]) + (after[...] + before[...])
    for peer in range(PEERS):
        out[peer] = summed


def place_kernel(flip, places, rows, *refs):
    gain_before = refs[0] if flip else None
    conv_hbm, head_hbm, gain_out, sems = refs[3:7] if flip else refs
    wide = C // 128
    half = 1 - places[1] if flip else places[1]
    copies = []
    for block in range(HALF):
        at = half * HALF + block
        tap = at >> 2
        lanes = pl.ds(pl.multiple_of((at & 3) * 128, 128), 128)
        source = rows.at[:, pl.ds(block * EACH, EACH), :]
        copies.append(pltpu.make_async_copy(source, conv_hbm.at[tap, :, :, lanes], sems.at[block]))
    source = rows.at[:, pl.ds(CONV_ROWS, PROJ_ROWS), :]
    copies.append(pltpu.make_async_copy(source, head_hbm.at[half], sems.at[HALF]))
    for copy in copies:
        copy.start()
    summed = rows[0, CHUNK:, :]
    for peer in range(1, PEERS):
        summed = summed + rows[peer, CHUNK:, :]
    if flip:
        gain_sum = refs[7]
        gain_sum[...] = (summed + gain_before[...])[0:wide, :]
        copies.append(pltpu.make_async_copy(gain_sum, gain_out, sems.at[HALF + 1]))
        copies[-1].start()
    else:
        gain_out[...] = summed
    for copy in copies:
        copy.wait()


def place(flip, places, rows, before=None):
    f32 = jnp.float32
    return pl.pallas_call(
        functools.partial(place_kernel, flip),
        in_specs=[IN_SMEM, IN_VMEM] + ([IN_VMEM, IN_HBM, IN_HBM] if flip else []),
        out_specs=[IN_HBM, IN_HBM, IN_HBM if flip else IN_VMEM],
        out_shape=(
            jax.ShapeDtypeStruct((TAPS, PEERS, EACH, C), f32),
            jax.ShapeDtypeStruct((2, PEERS, PROJ_ROWS, PROJ), f32),
            jax.ShapeDtypeStruct((C // 128 if flip else GAIN_ROWS, 128), f32),
        ),
        scratch_shapes=[DMA((HALF + 2,))] + ([VMEM((C // 128, 128), f32)] if flip else []),
        input_output_aliases={3: 0, 4: 1} if flip else {},
        compiler_params=pltpu.CompilerParams(vmem_limit_bytes=24 << 20),
        cost_estimate=pl.CostEstimate(flops=1 << 20, bytes_accessed=4 << 20, transcendentals=0),
        name="place_other" if flip else "place_mine",
    )(places, rows, *((before[2], before[0], before[1]) if flip else ()))


def body(segments, conv_weight, gain, head, group, positive):
    f32 = jnp.float32
    peers = ("x", "yh", "zl", "yl")
    swap = [(0, 1), (1, 0)]
    places = jnp.stack([lax.axis_index(("x", "yh")), lax.axis_index("core")]).astype(jnp.int32)
    normed, slope, pack, send = forward(group, positive, segments, conv_weight, gain.reshape(1, C), head)
    gathered = lax.all_to_all(send, ("x", "yh"), 0, 0)
    pack = jnp.where(places[1] >= 0, pack, 0.0)
    grad, keep, give = weight_gradient(places, gathered, pack, normed, slope)
    received = lax.ppermute(give, "core", swap)
    gain_part = gain_gradient(grad, segments, conv_weight)
    paired, gain_part = small_call(
        pair_sum_kernel,
        (jax.ShapeDtypeStruct((PEERS, CHUNK, 128), f32), jax.ShapeDtypeStruct((GAIN_ROWS, 128), f32)),
        "pair_sum",
        keep,
        received,
        gain_part,
    )
    across = lax.all_to_all(paired, peers, 0, 0)
    chunk = small_call(peer_sum_kernel, jax.ShapeDtypeStruct((LONG, 128), f32), "peer_sum", across, gain_part)
    rings = [lax.ppermute(chunk, "zh", [(i, (i + d) % STACKS) for i in range(STACKS)]) for d in (1, 2, 3)]
    spread = small_call(
        stack_sum_kernel, jax.ShapeDtypeStruct((PEERS, LONG, 128), f32), "stack_sum", chunk, *rings
    )
    mine = lax.all_to_all(spread, peers, 0, 0)
    other = lax.ppermute(mine, "core", swap)
    conv_grad, head_grad, gain_grad = place(True, places, other, place(False, places, mine))
    return conv_grad.reshape(TAPS, C, C), gain_grad.reshape(C), head_grad.reshape(C, PROJ)


def solution(mesh):
    fine = Mesh(mesh.devices.reshape(4, 2, 4, 2, 2, 2), ("x", "yh", "zh", "zl", "yl", "core"))
    row, grp = ("x", "yh"), ("zh", "zl", "yl", "core")
    placed = (P(grp, row, None, None), P(), P(), P(), P(grp, row), P(grp, row))
    return jax.shard_map(body, mesh=fine, in_specs=placed, out_specs=(P(), P(), P()), check_vma=False)
```

```python
import functools

import jax
import jax.numpy as jnp
from jax import lax
from jax.experimental import pallas as pl
from jax.experimental.pallas import tpu as pltpu
from jax.sharding import Mesh, PartitionSpec as P

GAP = 2
TEMPERATURE = 0.1
EPS = 1e-05
HIGHEST = lax.Precision.HIGHEST

SEGS = 16
LEN = 128
C = 512
PROJ = 128
TAPS = 3
STEP_SEGS = 8
F_STEP = 4
F_STEPS = SEGS // F_STEP
F_JOIN = 4
ROWS = STEP_SEGS * LEN
STEPS = SEGS // STEP_SEGS
JOIN = 2

RANKS = 8
PEERS = 32
STACKS = 4
BLOCKS = TAPS * C // 128
HALF = BLOCKS // 2
EACH = C // PEERS
CONV_ROWS = HALF * EACH
PROJ_ROWS = C // 2 // PEERS
CHUNK = CONV_ROWS + PROJ_ROWS
GAIN_ROWS = 8
LONG = CHUNK + GAIN_ROWS

PACK_POOLED = 2 * SEGS
PACK_HEAD = PACK_POOLED + SEGS * C // 128
PACK = PACK_HEAD + C

VMEM = pltpu.VMEM
SMEM = pltpu.SMEM
DMA = pltpu.SemaphoreType.DMA
IN_HBM = pl.BlockSpec(memory_space=pl.ANY)
FULL = 67043328
IN_VMEM = pl.BlockSpec(memory_space=VMEM)
IN_SMEM = pl.BlockSpec(memory_space=SMEM)


def whole(shape, space=None):
    zeros = (0,) * len(shape)
    return pl.BlockSpec(shape, lambda *_: zeros, memory_space=space)


def later(rows):
    return jnp.concatenate([rows[GAP:], jnp.zeros((GAP, rows.shape[1]), rows.dtype)], axis=0)


def earlier(rows):
    return jnp.concatenate([jnp.zeros((GAP, rows.shape[1]), rows.dtype), rows[:-GAP]], axis=0)


def unit_rows(values):
    return values * lax.rsqrt(jnp.mean(values * values, axis=-1, keepdims=True) + EPS)


def forward_kernel(
    group_hbm, positive_hbm, segments_hbm, weight_hbm, gain_hbm, head_hbm,
    normed_hbm, slope_hbm, pack_hbm, send_hbm,
    group, positive, segments, weight, gain, head, pooled, normed_out, slope_out, pack_out, send_out,
    step_sems, out_sems, sems,
):
    cubic = 0.044715
    scale = 0.7978845608028654

    def fetch(step):
        span = pl.ds(step * F_STEP, F_STEP)
        return pltpu.make_async_copy(segments_hbm.at[0, span], segments.at[span], step_sems.at[step])

    def store(step):
        span = pl.ds(step * F_STEP, F_STEP)
        return (
            pltpu.make_async_copy(normed_out.at[span], normed_hbm.at[span], out_sems.at[0, step]),
            pltpu.make_async_copy(slope_out.at[span], slope_hbm.at[span], out_sems.at[1, step]),
        )

    gain_copy = pltpu.make_async_copy(gain_hbm, gain, sems.at[0])
    weight_copy = pltpu.make_async_copy(weight_hbm, weight, sems.at[1])
    head_copy = pltpu.make_async_copy(head_hbm, head, sems.at[2])
    group_copy = pltpu.make_async_copy(group_hbm, group, sems.at[3])
    positive_copy = pltpu.make_async_copy(positive_hbm, positive, sems.at[4])
    start_rows, head_rows = pl.ds(0, PACK_HEAD), pl.ds(PACK_HEAD, C)
    head_store = pltpu.make_async_copy(pack_out.at[head_rows], pack_hbm.at[head_rows], sems.at[5])
    pack_store = pltpu.make_async_copy(pack_out.at[start_rows], pack_hbm.at[start_rows], sems.at[6])
    send_store = pltpu.make_async_copy(send_out, send_hbm, sems.at[7])
    gain_copy.start()
    fetch(0).start()
    weight_copy.start()
    for step in range(1, F_STEPS):
        fetch(step).start()
    head_copy.start()
    group_copy.start()
    positive_copy.start()
    gain_copy.wait()

    def one_step(step, carry):
        fetch(step).wait()

        @pl.when(step == 0)
        def _():
            weight_copy.wait()

        for first in range(0, F_STEP, F_JOIN):
            wide = []
            for index in range(first, first + F_JOIN):
                segment = step * F_STEP + index
                normed = (unit_rows(segments[segment].astype(jnp.float32)) * gain[...]).astype(jnp.bfloat16)
                normed_out[segment] = normed
                wide.append(jnp.concatenate([earlier(normed), normed, later(normed)], axis=1))
            joined = jnp.dot(jnp.concatenate(wide, axis=0), weight[...], preferred_element_type=jnp.float32)
            for index in range(first, first + F_JOIN):
                segment = step * F_STEP + index
                inputs = segments[segment].astype(jnp.float32)
                conv = joined[(index - first) * LEN : (index - first + 1) * LEN]
                square = conv * conv
                bent = jnp.tanh(conv * (scale + (scale * cubic) * square))
                half = 0.5 + 0.5 * bent
                hidden = inputs + conv * half
                slope_out[segment] = half + (0.5 * conv) * (1.0 - bent * bent) * (
                    scale + (3.0 * scale * cubic) * square
                )
                pooled[pl.ds(segment, 1), :] = jnp.sum(hidden, axis=0, keepdims=True) * (1.0 / LEN)
        for copy in store(step):
            copy.start()
        return carry

    lax.fori_loop(0, F_STEPS, one_step, 0)
    head_copy.wait()
    pack_out[PACK_HEAD:, :] = head[...].astype(jnp.float32)
    head_store.start()
    group_copy.wait()
    positive_copy.wait()
    rounded = pooled[...].astype(jnp.bfloat16)
    projected = jnp.dot(rounded, head[...], preferred_element_type=jnp.float32)
    pack_out[0:SEGS, :] = projected
    for index in range(SEGS):
        row = jnp.full((1, PROJ), positive[0, index], jnp.int32)
        pack_out[SEGS + index : SEGS + index + 1, :] = row.astype(jnp.float32)
    for block in range(C // 128):
        at = PACK_POOLED + block * SEGS
        pack_out[at : at + SEGS, :] = rounded[:, block * 128 : (block + 1) * 128].astype(jnp.float32)
    embedding = unit_rows(projected) * PROJ ** (-0.5)
    lane = lax.broadcasted_iota(jnp.int32, (8, 128), 1) & (SEGS - 1)
    groups = jnp.zeros((8, 128), jnp.int32)
    for index in range(SEGS):
        groups = jnp.where(lane == index, group[0, index], groups)
    groups = groups.astype(jnp.float32)
    for rank in range(RANKS):
        send_out[rank, 0:SEGS, :] = embedding
        send_out[rank, SEGS:, :] = groups
    send_store.start()
    pack_store.start()
    head_store.wait()
    send_store.wait()
    pack_store.wait()
    for step in range(F_STEPS):
        for copy in store(step):
            copy.wait()


def forward(group, positive, segments, weight, gain, head):
    f32 = jnp.float32
    bf16 = jnp.bfloat16
    return pl.pallas_call(
        forward_kernel,
        in_specs=[IN_HBM] * 6,
        out_specs=[IN_HBM] * 4,
        out_shape=[
            jax.ShapeDtypeStruct((SEGS, LEN, C), bf16),
            jax.ShapeDtypeStruct((SEGS, LEN, C), f32),
            jax.ShapeDtypeStruct((PACK, PROJ), f32),
            jax.ShapeDtypeStruct((RANKS, SEGS + 8, PROJ), f32),
        ],
        scratch_shapes=[
            SMEM((1, SEGS), jnp.int32),
            SMEM((1, SEGS), jnp.int32),
            VMEM((SEGS, LEN, C), bf16),
            VMEM((TAPS * C, C), bf16),
            VMEM((1, C), f32),
            VMEM((C, PROJ), bf16),
            VMEM((SEGS, C), f32),
            VMEM((SEGS, LEN, C), bf16),
            VMEM((SEGS, LEN, C), f32),
            VMEM((PACK, PROJ), f32),
            VMEM((RANKS, SEGS + 8, PROJ), f32),
            DMA((F_STEPS,)),
            DMA((2, F_STEPS)),
            DMA((8,)),
        ],
        compiler_params=pltpu.CompilerParams(vmem_limit_bytes=FULL),
        cost_estimate=pl.CostEstimate(flops=2 * SEGS * LEN * TAPS * C * C, bytes_accessed=10 << 20, transcendentals=SEGS * LEN * C),
        name="forward",
    )(group, positive, segments, weight.reshape(TAPS * C, C), gain, head)


def loss_gradient(gathered, pack, place):
    projected = pack[0:SEGS, :]
    pooled = jnp.concatenate(
        [pack[PACK_POOLED + block * SEGS : PACK_POOLED + (block + 1) * SEGS, :] for block in range(C // 128)], axis=1
    )
    embeddings = gathered[:, 0:SEGS, :].reshape(RANKS * SEGS, PROJ)
    own = unit_rows(projected) * PROJ ** (-0.5)
    count = RANKS * SEGS
    nt = (((1,), (1,)), ((), ()))
    lane = lax.broadcasted_iota(jnp.int32, (8, 128), 1)
    groups = jnp.zeros((8, 128), jnp.float32)
    for rank in range(RANKS):
        groups = jnp.where(lane >> 4 == rank, gathered[rank, SEGS:, :], groups)
    by_column = jnp.broadcast_to(groups[0:1], (count, count))
    by_row = by_column.T
    row = lax.broadcasted_iota(jnp.int32, (count, count), 0)
    column = lax.broadcasted_iota(jnp.int32, (count, count), 1)
    same = (by_row == by_column) & (row != column)
    scores = lax.dot_general(
        embeddings, embeddings, nt, precision=HIGHEST, preferred_element_type=jnp.float32
    ) / TEMPERATURE
    column_total = jnp.log(jnp.sum(jnp.where(same, jnp.exp(scores), 0.0), axis=0, keepdims=True))

    own_scores = lax.dot_general(
        own, embeddings, nt, precision=HIGHEST, preferred_element_type=jnp.float32
    ) / TEMPERATURE
    own_row = lax.broadcasted_iota(jnp.int32, (SEGS, count), 0) + place * SEGS
    own_column = lax.broadcasted_iota(jnp.int32, (SEGS, count), 1)
    own_group = jnp.sum(jnp.where(own_row == own_column, groups[0:1], 0.0), axis=1, keepdims=True)
    own_same = (own_group == groups[0:1]) & (own_row != own_column)
    own_total = jnp.log(jnp.sum(jnp.where(own_same, jnp.exp(own_scores), 0.0), axis=1, keepdims=True))
    both = jnp.where(own_same, jnp.exp(own_scores - own_total) + jnp.exp(own_scores - column_total), 0.0)
    pulled = jnp.dot(both, embeddings, precision=HIGHEST, preferred_element_type=jnp.float32)
    picked = (pack[SEGS : 2 * SEGS, :] == own_column.astype(jnp.float32)).astype(jnp.float32)
    partner = jnp.dot(picked, embeddings, precision=HIGHEST, preferred_element_type=jnp.float32)
    factor = (count * 32) ** (-0.5) / TEMPERATURE
    embed_grad = factor * (pulled - 2.0 * partner)

    values = projected
    inverse = lax.rsqrt(jnp.mean(values * values, axis=-1, keepdims=True) + EPS)
    outer = embed_grad * PROJ ** (-0.5)
    dotted = jnp.mean(values * outer, axis=-1, keepdims=True)
    projected_grad = inverse * outer - values * (inverse * inverse * inverse * dotted)
    derivative = lax.dot_general(
        pooled,
        projected_grad,
        (((0,), (0,)), ((), ())),
        precision=HIGHEST,
        preferred_element_type=jnp.float32,
    )
    hidden_grad = lax.dot_general(
        projected_grad, pack[PACK_HEAD:, :], nt, precision=HIGHEST, preferred_element_type=jnp.float32
    ) * (1.0 / LEN)
    return derivative, hidden_grad


def weight_kernel(
    places, gathered, pack, normed_hbm, slope_hbm,
    grad_hbm, keep_out, send_out,
    total, hidden_grad, derivative, normed, slope, grad_out, step_sems,
):
    def fetch(step):
        span = pl.ds(step * STEP_SEGS, STEP_SEGS)
        return (
            pltpu.make_async_copy(slope_hbm.at[span], slope.at[span], step_sems.at[0, step]),
            pltpu.make_async_copy(normed_hbm.at[span], normed.at[span], step_sems.at[1, step]),
        )

    def store(step):
        span = pl.ds(step * STEP_SEGS, STEP_SEGS)
        return pltpu.make_async_copy(grad_out.at[span], grad_hbm.at[span], step_sems.at[2, step])

    for step in range(STEPS):
        for copy in fetch(step):
            copy.start()
    derivative[...], hidden_grad[...] = loss_gradient(gathered, pack, places[0])
    total[...] = jnp.zeros_like(total)

    def one_step(step, carry):
        for copy in fetch(step):
            copy.wait()
        sides = []
        for index in range(STEP_SEGS):
            segment = step * STEP_SEGS + index
            grad = (hidden_grad[pl.ds(segment, 1), :] * slope[segment]).astype(jnp.bfloat16)
            grad_out[segment] = grad
            sides.append(jnp.concatenate([later(grad), grad, earlier(grad)], axis=1))
        rows = normed[pl.ds(step * STEP_SEGS, STEP_SEGS)].reshape(ROWS, C)
        product = lax.dot_general(
            rows, jnp.concatenate(sides, axis=0), (((0,), (0,)), ((), ())), preferred_element_type=jnp.float32
        )
        for block in range(BLOCKS):
            total[block] += product[:, block * 128 : (block + 1) * 128]
        store(step).start()
        return carry

    lax.fori_loop(0, STEPS, one_step, 0)
    core = places[1]
    for target, which in ((keep_out, core), (send_out, 1 - core)):
        for peer in range(PEERS):
            for block in range(HALF):
                target[peer, block * EACH : (block + 1) * EACH, :] = total[
                    which * HALF + block, peer * EACH : (peer + 1) * EACH, :
                ]
            target[peer, CONV_ROWS:, :] = derivative[
                pl.ds(pl.multiple_of(which * (C // 2) + peer * PROJ_ROWS, PROJ_ROWS), PROJ_ROWS), :
            ]
    for step in range(STEPS):
        store(step).wait()


def weight_gradient(places, gathered, pack, normed, slope):
    f32 = jnp.float32
    bf16 = jnp.bfloat16
    return pl.pallas_call(
        weight_kernel,
        in_specs=[IN_SMEM, IN_VMEM, IN_VMEM, IN_HBM, IN_HBM],
        out_specs=[IN_HBM] + [IN_VMEM] * 2,
        out_shape=[
            jax.ShapeDtypeStruct((SEGS, LEN, C), bf16),
            jax.ShapeDtypeStruct((PEERS, CHUNK, 128), f32),
            jax.ShapeDtypeStruct((PEERS, CHUNK, 128), f32),
        ],
        scratch_shapes=[
            VMEM((BLOCKS, C, 128), f32),
            VMEM((SEGS, C), f32),
            VMEM((C, PROJ), f32),
            VMEM((SEGS, LEN, C), bf16),
            VMEM((SEGS, LEN, C), f32),
            VMEM((SEGS, LEN, C), bf16),
            DMA((3, STEPS)),
        ],
        compiler_params=pltpu.CompilerParams(vmem_limit_bytes=48 << 20),
        cost_estimate=pl.CostEstimate(flops=2 * SEGS * LEN * TAPS * C * C, bytes_accessed=12 << 20, transcendentals=1 << 16),
        name="weight_gradient",
    )(places, gathered, pack, normed, slope)


def gain_kernel(grad, segments, weight, out, total, wide):
    step = pl.program_id(0)

    @pl.when(step == 0)
    def _():
        total[...] = jnp.zeros_like(total)
        for tap in range(TAPS):
            wide[:, tap * C : (tap + 1) * C] = weight[tap]

    for first in range(0, STEP_SEGS, JOIN):
        sides = []
        for index in range(first, first + JOIN):
            middle = grad[index]
            sides.append(jnp.concatenate([later(middle), middle, earlier(middle)], axis=1))
        joined = lax.dot_general(
            jnp.concatenate(sides, axis=0), wide[...], (((1,), (1,)), ((), ())), preferred_element_type=jnp.float32
        )
        for index in range(first, first + JOIN):
            product = joined[(index - first) * LEN : (index - first + 1) * LEN] * unit_rows(
                segments[0, index].astype(jnp.float32)
            )
            total[...] += jnp.sum(product.reshape(LEN // 8, 8, C), axis=0)

    @pl.when(step == STEPS - 1)
    def _():
        summed = jnp.sum(total[...], axis=0, keepdims=True)
        for block in range(GAIN_ROWS):
            at = block % (C // 128)
            out[block : block + 1, :] = summed[:, at * 128 : (at + 1) * 128]


def gain_gradient(grad, segments, weight):
    f32 = jnp.float32
    return pl.pallas_call(
        gain_kernel,
        grid=(STEPS,),
        in_specs=[
            pl.BlockSpec((STEP_SEGS, LEN, C), lambda i: (i, 0, 0)),
            pl.BlockSpec((1, STEP_SEGS, LEN, C), lambda i: (0, i, 0, 0)),
            whole((TAPS, C, C)),
        ],
        out_specs=whole((GAIN_ROWS, 128)),
        out_shape=jax.ShapeDtypeStruct((GAIN_ROWS, 128), f32),
        scratch_shapes=[VMEM((8, C), f32), VMEM((C, TAPS * C), jnp.bfloat16)],
        compiler_params=pltpu.CompilerParams(vmem_limit_bytes=32 << 20),
        cost_estimate=pl.CostEstimate(flops=2 * SEGS * LEN * TAPS * C * C, bytes_accessed=6 << 20, transcendentals=0),
        name="gain_gradient",
    )(grad, segments, weight)


def small_call(body, out_shape, name, *args):
    return pl.pallas_call(
        body,
        out_shape=out_shape,
        compiler_params=pltpu.CompilerParams(vmem_limit_bytes=24 << 20),
        cost_estimate=pl.CostEstimate(flops=1 << 20, bytes_accessed=4 << 20, transcendentals=0),
        name=name,
    )(*args)


def pair_sum_kernel(keep, received, gain, out, gain_out):
    gain_out[...] = gain[...]
    for peer in range(PEERS):
        out[peer] = keep[peer] + received[peer]


def peer_sum_kernel(received, gain, out):
    summed = received[0]
    for source in range(1, PEERS):
        summed = summed + received[source]
    out[0:CHUNK, :] = summed
    out[CHUNK:, :] = gain[...]


def stack_sum_kernel(own, after, across, before, out):
    summed = (own[...] + across[...]) + (after[...] + before[...])
    for peer in range(PEERS):
        out[peer] = summed


def place_kernel(flip, places, rows, *refs):
    gain_before = refs[0] if flip else None
    conv_hbm, head_hbm, gain_out, sems = refs[3:7] if flip else refs
    wide = C // 128
    half = 1 - places[1] if flip else places[1]
    copies = []
    for block in range(HALF):
        at = half * HALF + block
        tap = at >> 2
        lanes = pl.ds(pl.multiple_of((at & 3) * 128, 128), 128)
        source = rows.at[:, pl.ds(block * EACH, EACH), :]
        copies.append(pltpu.make_async_copy(source, conv_hbm.at[tap, :, :, lanes], sems.at[block]))
    source = rows.at[:, pl.ds(CONV_ROWS, PROJ_ROWS), :]
    copies.append(pltpu.make_async_copy(source, head_hbm.at[half], sems.at[HALF]))
    for copy in copies:
        copy.start()
    summed = rows[0, CHUNK:, :]
    for peer in range(1, PEERS):
        summed = summed + rows[peer, CHUNK:, :]
    if flip:
        gain_sum = refs[7]
        gain_sum[...] = (summed + gain_before[...])[0:wide, :]
        copies.append(pltpu.make_async_copy(gain_sum, gain_out, sems.at[HALF + 1]))
        copies[-1].start()
    else:
        gain_out[...] = summed
    for copy in copies:
        copy.wait()


def place(flip, places, rows, before=None):
    f32 = jnp.float32
    return pl.pallas_call(
        functools.partial(place_kernel, flip),
        in_specs=[IN_SMEM, IN_VMEM] + ([IN_VMEM, IN_HBM, IN_HBM] if flip else []),
        out_specs=[IN_HBM, IN_HBM, IN_HBM if flip else IN_VMEM],
        out_shape=(
            jax.ShapeDtypeStruct((TAPS, PEERS, EACH, C), f32),
            jax.ShapeDtypeStruct((2, PEERS, PROJ_ROWS, PROJ), f32),
            jax.ShapeDtypeStruct((C // 128 if flip else GAIN_ROWS, 128), f32),
        ),
        scratch_shapes=[DMA((HALF + 2,))] + ([VMEM((C // 128, 128), f32)] if flip else []),
        input_output_aliases={3: 0, 4: 1} if flip else {},
        compiler_params=pltpu.CompilerParams(vmem_limit_bytes=24 << 20),
        cost_estimate=pl.CostEstimate(flops=1 << 20, bytes_accessed=4 << 20, transcendentals=0),
        name="place_other" if flip else "place_mine",
    )(places, rows, *((before[2], before[0], before[1]) if flip else ()))


def body(segments, conv_weight, gain, head, group, positive):
    f32 = jnp.float32
    peers = ("zl", "yh", "yl", "x")
    swap = [(0, 1), (1, 0)]
    places = jnp.stack([lax.axis_index(("x", "yh")), lax.axis_index("core")]).astype(jnp.int32)
    normed, slope, pack, send = forward(group, positive, segments, conv_weight, gain.reshape(1, C), head)
    gathered = lax.all_to_all(send, ("x", "yh"), 0, 0)
    pack = jnp.where(places[1] >= 0, pack, 0.0)
    grad, keep, give = weight_gradient(places, gathered, pack, normed, slope)
    received = lax.ppermute(give, "core", swap)
    gain_part = gain_gradient(grad, segments, conv_weight)
    paired, gain_part = small_call(
        pair_sum_kernel,
        (jax.ShapeDtypeStruct((PEERS, CHUNK, 128), f32), jax.ShapeDtypeStruct((GAIN_ROWS, 128), f32)),
        "pair_sum",
        keep,
        received,
        gain_part,
    )
    across = lax.all_to_all(paired, peers, 0, 0)
    chunk = small_call(peer_sum_kernel, jax.ShapeDtypeStruct((LONG, 128), f32), "peer_sum", across, gain_part)
    rings = [lax.ppermute(chunk, "zh", [(i, (i + d) % STACKS) for i in range(STACKS)]) for d in (1, 2, 3)]
    spread = small_call(
        stack_sum_kernel, jax.ShapeDtypeStruct((PEERS, LONG, 128), f32), "stack_sum", chunk, *rings
    )
    mine = lax.all_to_all(spread, peers, 0, 0)
    other = lax.ppermute(mine, "core", swap)
    conv_grad, head_grad, gain_grad = place(True, places, other, place(False, places, mine))
    return conv_grad.reshape(TAPS, C, C), gain_grad.reshape(C), head_grad.reshape(C, PROJ)


def solution(mesh):
    fine = Mesh(mesh.devices.reshape(4, 2, 4, 2, 2, 2), ("x", "yh", "zh", "zl", "yl", "core"))
    row, grp = ("x", "yh"), ("zh", "zl", "yl", "core")
    placed = (P(grp, row, None, None), P(), P(), P(), P(grp, row), P(grp, row))
    return jax.shard_map(body, mesh=fine, in_specs=placed, out_specs=(P(), P(), P()), check_vma=False)
```

```python
import functools

import jax
import jax.numpy as jnp
from jax import lax
from jax.experimental import pallas as pl
from jax.experimental.pallas import tpu as pltpu
from jax.sharding import Mesh, PartitionSpec as P

GAP = 2
TEMPERATURE = 0.1
EPS = 1e-05
HIGHEST = lax.Precision.HIGHEST

SEGS = 16
LEN = 128
C = 512
PROJ = 128
TAPS = 3
STEP_SEGS = 8
F_STEP = 4
F_STEPS = SEGS // F_STEP
F_JOIN = 4
ROWS = STEP_SEGS * LEN
STEPS = SEGS // STEP_SEGS
JOIN = 2

RANKS = 8
PEERS = 32
STACKS = 4
BLOCKS = TAPS * C // 128
HALF = BLOCKS // 2
EACH = C // PEERS
CONV_ROWS = HALF * EACH
PROJ_ROWS = C // 2 // PEERS
CHUNK = CONV_ROWS + PROJ_ROWS
GAIN_ROWS = 8
LONG = CHUNK + GAIN_ROWS

PACK_POOLED = 2 * SEGS
PACK_HEAD = PACK_POOLED + SEGS * C // 128
PACK = PACK_HEAD + C

VMEM = pltpu.VMEM
SMEM = pltpu.SMEM
DMA = pltpu.SemaphoreType.DMA
IN_HBM = pl.BlockSpec(memory_space=pl.ANY)
FULL = 67043328
IN_VMEM = pl.BlockSpec(memory_space=VMEM)
IN_SMEM = pl.BlockSpec(memory_space=SMEM)


def whole(shape, space=None):
    zeros = (0,) * len(shape)
    return pl.BlockSpec(shape, lambda *_: zeros, memory_space=space)


def later(rows):
    return jnp.concatenate([rows[GAP:], jnp.zeros((GAP, rows.shape[1]), rows.dtype)], axis=0)


def earlier(rows):
    return jnp.concatenate([jnp.zeros((GAP, rows.shape[1]), rows.dtype), rows[:-GAP]], axis=0)


def unit_rows(values):
    return values * lax.rsqrt(jnp.mean(values * values, axis=-1, keepdims=True) + EPS)


def forward_kernel(
    group_hbm, positive_hbm, segments_hbm, weight_hbm, gain_hbm, head_hbm,
    normed_hbm, slope_hbm, pack_hbm, send_hbm,
    group, positive, segments, weight, gain, head, pooled, normed_out, slope_out, pack_out, send_out,
    step_sems, out_sems, sems,
):
    cubic = 0.044715
    scale = 0.7978845608028654

    def fetch(step):
        span = pl.ds(step * F_STEP, F_STEP)
        return pltpu.make_async_copy(segments_hbm.at[0, span], segments.at[span], step_sems.at[step])

    def store(step):
        span = pl.ds(step * F_STEP, F_STEP)
        return (
            pltpu.make_async_copy(normed_out.at[span], normed_hbm.at[span], out_sems.at[0, step]),
            pltpu.make_async_copy(slope_out.at[span], slope_hbm.at[span], out_sems.at[1, step]),
        )

    gain_copy = pltpu.make_async_copy(gain_hbm, gain, sems.at[0])
    weight_copy = pltpu.make_async_copy(weight_hbm, weight, sems.at[1])
    head_copy = pltpu.make_async_copy(head_hbm, head, sems.at[2])
    group_copy = pltpu.make_async_copy(group_hbm, group, sems.at[3])
    positive_copy = pltpu.make_async_copy(positive_hbm, positive, sems.at[4])
    start_rows, head_rows = pl.ds(0, PACK_HEAD), pl.ds(PACK_HEAD, C)
    head_store = pltpu.make_async_copy(pack_out.at[head_rows], pack_hbm.at[head_rows], sems.at[5])
    pack_store = pltpu.make_async_copy(pack_out.at[start_rows], pack_hbm.at[start_rows], sems.at[6])
    send_store = pltpu.make_async_copy(send_out, send_hbm, sems.at[7])
    gain_copy.start()
    fetch(0).start()
    weight_copy.start()
    for step in range(1, F_STEPS):
        fetch(step).start()
    head_copy.start()
    group_copy.start()
    positive_copy.start()
    gain_copy.wait()

    def one_step(step, carry):
        fetch(step).wait()

        @pl.when(step == 0)
        def _():
            weight_copy.wait()

        for first in range(0, F_STEP, F_JOIN):
            wide = []
            for index in range(first, first + F_JOIN):
                segment = step * F_STEP + index
                normed = (unit_rows(segments[segment].astype(jnp.float32)) * gain[...]).astype(jnp.bfloat16)
                normed_out[segment] = normed
                wide.append(jnp.concatenate([earlier(normed), normed, later(normed)], axis=1))
            joined = jnp.dot(jnp.concatenate(wide, axis=0), weight[...], preferred_element_type=jnp.float32)
            for index in range(first, first + F_JOIN):
                segment = step * F_STEP + index
                inputs = segments[segment].astype(jnp.float32)
                conv = joined[(index - first) * LEN : (index - first + 1) * LEN]
                square = conv * conv
                bent = jnp.tanh(conv * (scale + (scale * cubic) * square))
                half = 0.5 + 0.5 * bent
                hidden = inputs + conv * half
                slope_out[segment] = half + (0.5 * conv) * (1.0 - bent * bent) * (
                    scale + (3.0 * scale * cubic) * square
                )
                pooled[pl.ds(segment, 1), :] = jnp.sum(hidden, axis=0, keepdims=True) * (1.0 / LEN)
        for copy in store(step):
            copy.start()
        return carry

    lax.fori_loop(0, F_STEPS, one_step, 0)
    head_copy.wait()
    pack_out[PACK_HEAD:, :] = head[...].astype(jnp.float32)
    head_store.start()
    group_copy.wait()
    positive_copy.wait()
    rounded = pooled[...].astype(jnp.bfloat16)
    projected = jnp.dot(rounded, head[...], preferred_element_type=jnp.float32)
    pack_out[0:SEGS, :] = projected
    for index in range(SEGS):
        other = positive[0, index]
        row = jnp.full((1, PROJ), ((other >> 4) & 1) * 64 + (other >> 5) * SEGS + (other & (SEGS - 1)), jnp.int32)
        pack_out[SEGS + index : SEGS + index + 1, :] = row.astype(jnp.float32)
    for block in range(C // 128):
        at = PACK_POOLED + block * SEGS
        pack_out[at : at + SEGS, :] = rounded[:, block * 128 : (block + 1) * 128].astype(jnp.float32)
    embedding = unit_rows(projected) * PROJ ** (-0.5)
    lane = lax.broadcasted_iota(jnp.int32, (8, 128), 1) & (SEGS - 1)
    groups = jnp.zeros((8, 128), jnp.int32)
    for index in range(SEGS):
        groups = jnp.where(lane == index, group[0, index], groups)
    groups = groups.astype(jnp.float32)
    for rank in range(RANKS):
        send_out[rank, 0:SEGS, :] = embedding
        send_out[rank, SEGS:, :] = groups
    send_store.start()
    pack_store.start()
    head_store.wait()
    send_store.wait()
    pack_store.wait()
    for step in range(F_STEPS):
        for copy in store(step):
            copy.wait()


def forward(group, positive, segments, weight, gain, head):
    f32 = jnp.float32
    bf16 = jnp.bfloat16
    return pl.pallas_call(
        forward_kernel,
        in_specs=[IN_HBM] * 6,
        out_specs=[IN_HBM] * 4,
        out_shape=[
            jax.ShapeDtypeStruct((SEGS, LEN, C), bf16),
            jax.ShapeDtypeStruct((SEGS, LEN, C), f32),
            jax.ShapeDtypeStruct((PACK, PROJ), f32),
            jax.ShapeDtypeStruct((RANKS, SEGS + 8, PROJ), f32),
        ],
        scratch_shapes=[
            SMEM((1, SEGS), jnp.int32),
            SMEM((1, SEGS), jnp.int32),
            VMEM((SEGS, LEN, C), bf16),
            VMEM((TAPS * C, C), bf16),
            VMEM((1, C), f32),
            VMEM((C, PROJ), bf16),
            VMEM((SEGS, C), f32),
            VMEM((SEGS, LEN, C), bf16),
            VMEM((SEGS, LEN, C), f32),
            VMEM((PACK, PROJ), f32),
            VMEM((RANKS, SEGS + 8, PROJ), f32),
            DMA((F_STEPS,)),
            DMA((2, F_STEPS)),
            DMA((8,)),
        ],
        compiler_params=pltpu.CompilerParams(vmem_limit_bytes=FULL),
        cost_estimate=pl.CostEstimate(flops=2 * SEGS * LEN * TAPS * C * C, bytes_accessed=10 << 20, transcendentals=SEGS * LEN * C),
        name="forward",
    )(group, positive, segments, weight.reshape(TAPS * C, C), gain, head)


def loss_gradient(gathered, pack, place):
    projected = pack[0:SEGS, :]
    pooled = jnp.concatenate(
        [pack[PACK_POOLED + block * SEGS : PACK_POOLED + (block + 1) * SEGS, :] for block in range(C // 128)], axis=1
    )
    embeddings = gathered[:, 0:SEGS, :].reshape(RANKS * SEGS, PROJ)
    own = unit_rows(projected) * PROJ ** (-0.5)
    count = RANKS * SEGS
    nt = (((1,), (1,)), ((), ()))
    lane = lax.broadcasted_iota(jnp.int32, (8, 128), 1)
    groups = jnp.zeros((8, 128), jnp.float32)
    for rank in range(RANKS):
        groups = jnp.where(lane >> 4 == rank, gathered[rank, SEGS:, :], groups)
    by_column = jnp.broadcast_to(groups[0:1], (count, count))
    by_row = by_column.T
    row = lax.broadcasted_iota(jnp.int32, (count, count), 0)
    column = lax.broadcasted_iota(jnp.int32, (count, count), 1)
    same = (by_row == by_column) & (row != column)
    scores = lax.dot_general(
        embeddings, embeddings, nt, precision=HIGHEST, preferred_element_type=jnp.float32
    ) / TEMPERATURE
    column_total = jnp.log(jnp.sum(jnp.where(same, jnp.exp(scores), 0.0), axis=0, keepdims=True))

    own_scores = lax.dot_general(
        own, embeddings, nt, precision=HIGHEST, preferred_element_type=jnp.float32
    ) / TEMPERATURE
    own_row = lax.broadcasted_iota(jnp.int32, (SEGS, count), 0) + place * SEGS
    own_column = lax.broadcasted_iota(jnp.int32, (SEGS, count), 1)
    own_group = jnp.sum(jnp.where(own_row == own_column, groups[0:1], 0.0), axis=1, keepdims=True)
    own_same = (own_group == groups[0:1]) & (own_row != own_column)
    own_total = jnp.log(jnp.sum(jnp.where(own_same, jnp.exp(own_scores), 0.0), axis=1, keepdims=True))
    both = jnp.where(own_same, jnp.exp(own_scores - own_total) + jnp.exp(own_scores - column_total), 0.0)
    pulled = jnp.dot(both, embeddings, precision=HIGHEST, preferred_element_type=jnp.float32)
    picked = (pack[SEGS : 2 * SEGS, :] == own_column.astype(jnp.float32)).astype(jnp.float32)
    partner = jnp.dot(picked, embeddings, precision=HIGHEST, preferred_element_type=jnp.float32)
    factor = (count * 32) ** (-0.5) / TEMPERATURE
    embed_grad = factor * (pulled - 2.0 * partner)

    values = projected
    inverse = lax.rsqrt(jnp.mean(values * values, axis=-1, keepdims=True) + EPS)
    outer = embed_grad * PROJ ** (-0.5)
    dotted = jnp.mean(values * outer, axis=-1, keepdims=True)
    projected_grad = inverse * outer - values * (inverse * inverse * inverse * dotted)
    derivative = lax.dot_general(
        pooled,
        projected_grad,
        (((0,), (0,)), ((), ())),
        precision=HIGHEST,
        preferred_element_type=jnp.float32,
    )
    hidden_grad = lax.dot_general(
        projected_grad, pack[PACK_HEAD:, :], nt, precision=HIGHEST, preferred_element_type=jnp.float32
    ) * (1.0 / LEN)
    return derivative, hidden_grad


def weight_kernel(
    places, gathered, pack, normed_hbm, slope_hbm,
    grad_hbm, keep_out, send_out,
    total, hidden_grad, derivative, normed, slope, grad_out, step_sems,
):
    def fetch(step):
        span = pl.ds(step * STEP_SEGS, STEP_SEGS)
        return (
            pltpu.make_async_copy(slope_hbm.at[span], slope.at[span], step_sems.at[0, step]),
            pltpu.make_async_copy(normed_hbm.at[span], normed.at[span], step_sems.at[1, step]),
        )

    def store(step):
        span = pl.ds(step * STEP_SEGS, STEP_SEGS)
        return pltpu.make_async_copy(grad_out.at[span], grad_hbm.at[span], step_sems.at[2, step])

    for step in range(STEPS):
        for copy in fetch(step):
            copy.start()
    derivative[...], hidden_grad[...] = loss_gradient(gathered, pack, places[0])
    total[...] = jnp.zeros_like(total)

    def one_step(step, carry):
        for copy in fetch(step):
            copy.wait()
        sides = []
        for index in range(STEP_SEGS):
            segment = step * STEP_SEGS + index
            grad = (hidden_grad[pl.ds(segment, 1), :] * slope[segment]).astype(jnp.bfloat16)
            grad_out[segment] = grad
            sides.append(jnp.concatenate([later(grad), grad, earlier(grad)], axis=1))
        rows = normed[pl.ds(step * STEP_SEGS, STEP_SEGS)].reshape(ROWS, C)
        product = lax.dot_general(
            rows, jnp.concatenate(sides, axis=0), (((0,), (0,)), ((), ())), preferred_element_type=jnp.float32
        )
        for block in range(BLOCKS):
            total[block] += product[:, block * 128 : (block + 1) * 128]
        store(step).start()
        return carry

    lax.fori_loop(0, STEPS, one_step, 0)
    core = places[1]
    for target, which in ((keep_out, core), (send_out, 1 - core)):
        for peer in range(PEERS):
            for block in range(HALF):
                target[peer, block * EACH : (block + 1) * EACH, :] = total[
                    which * HALF + block, peer * EACH : (peer + 1) * EACH, :
                ]
            target[peer, CONV_ROWS:, :] = derivative[
                pl.ds(pl.multiple_of(which * (C // 2) + peer * PROJ_ROWS, PROJ_ROWS), PROJ_ROWS), :
            ]
    for step in range(STEPS):
        store(step).wait()


def weight_gradient(places, gathered, pack, normed, slope):
    f32 = jnp.float32
    bf16 = jnp.bfloat16
    return pl.pallas_call(
        weight_kernel,
        in_specs=[IN_SMEM, IN_VMEM, IN_VMEM, IN_HBM, IN_HBM],
        out_specs=[IN_HBM] + [IN_VMEM] * 2,
        out_shape=[
            jax.ShapeDtypeStruct((SEGS, LEN, C), bf16),
            jax.ShapeDtypeStruct((PEERS, CHUNK, 128), f32),
            jax.ShapeDtypeStruct((PEERS, CHUNK, 128), f32),
        ],
        scratch_shapes=[
            VMEM((BLOCKS, C, 128), f32),
            VMEM((SEGS, C), f32),
            VMEM((C, PROJ), f32),
            VMEM((SEGS, LEN, C), bf16),
            VMEM((SEGS, LEN, C), f32),
            VMEM((SEGS, LEN, C), bf16),
            DMA((3, STEPS)),
        ],
        compiler_params=pltpu.CompilerParams(vmem_limit_bytes=48 << 20),
        cost_estimate=pl.CostEstimate(flops=2 * SEGS * LEN * TAPS * C * C, bytes_accessed=12 << 20, transcendentals=1 << 16),
        name="weight_gradient",
    )(places, gathered, pack, normed, slope)


def gain_kernel(grad, segments, weight, out, total, wide):
    step = pl.program_id(0)

    @pl.when(step == 0)
    def _():
        total[...] = jnp.zeros_like(total)
        for tap in range(TAPS):
            wide[:, tap * C : (tap + 1) * C] = weight[tap]

    for first in range(0, STEP_SEGS, JOIN):
        sides = []
        for index in range(first, first + JOIN):
            middle = grad[index]
            sides.append(jnp.concatenate([later(middle), middle, earlier(middle)], axis=1))
        joined = lax.dot_general(
            jnp.concatenate(sides, axis=0), wide[...], (((1,), (1,)), ((), ())), preferred_element_type=jnp.float32
        )
        for index in range(first, first + JOIN):
            product = joined[(index - first) * LEN : (index - first + 1) * LEN] * unit_rows(
                segments[0, index].astype(jnp.float32)
            )
            total[...] += jnp.sum(product.reshape(LEN // 8, 8, C), axis=0)

    @pl.when(step == STEPS - 1)
    def _():
        summed = jnp.sum(total[...], axis=0, keepdims=True)
        for block in range(GAIN_ROWS):
            at = block % (C // 128)
            out[block : block + 1, :] = summed[:, at * 128 : (at + 1) * 128]


def gain_gradient(grad, segments, weight):
    f32 = jnp.float32
    return pl.pallas_call(
        gain_kernel,
        grid=(STEPS,),
        in_specs=[
            pl.BlockSpec((STEP_SEGS, LEN, C), lambda i: (i, 0, 0)),
            pl.BlockSpec((1, STEP_SEGS, LEN, C), lambda i: (0, i, 0, 0)),
            whole((TAPS, C, C)),
        ],
        out_specs=whole((GAIN_ROWS, 128)),
        out_shape=jax.ShapeDtypeStruct((GAIN_ROWS, 128), f32),
        scratch_shapes=[VMEM((8, C), f32), VMEM((C, TAPS * C), jnp.bfloat16)],
        compiler_params=pltpu.CompilerParams(vmem_limit_bytes=32 << 20),
        cost_estimate=pl.CostEstimate(flops=2 * SEGS * LEN * TAPS * C * C, bytes_accessed=6 << 20, transcendentals=0),
        name="gain_gradient",
    )(grad, segments, weight)


def small_call(body, out_shape, name, *args):
    return pl.pallas_call(
        body,
        out_shape=out_shape,
        compiler_params=pltpu.CompilerParams(vmem_limit_bytes=24 << 20),
        cost_estimate=pl.CostEstimate(flops=1 << 20, bytes_accessed=4 << 20, transcendentals=0),
        name=name,
    )(*args)


def pair_sum_kernel(keep, received, gain, out, gain_out):
    gain_out[...] = gain[...]
    for peer in range(PEERS):
        out[peer] = keep[peer] + received[peer]


def peer_sum_kernel(received, gain, out):
    summed = received[0]
    for source in range(1, PEERS):
        summed = summed + received[source]
    out[0:CHUNK, :] = summed
    out[CHUNK:, :] = gain[...]


def stack_sum_kernel(own, after, across, before, out):
    summed = (own[...] + across[...]) + (after[...] + before[...])
    for peer in range(PEERS):
        out[peer] = summed


def place_kernel(flip, places, rows, *refs):
    gain_before = refs[0] if flip else None
    conv_hbm, head_hbm, gain_out, sems = refs[3:7] if flip else refs
    wide = C // 128
    half = 1 - places[1] if flip else places[1]
    copies = []
    for block in range(HALF):
        at = half * HALF + block
        tap = at >> 2
        lanes = pl.ds(pl.multiple_of((at & 3) * 128, 128), 128)
        source = rows.at[:, pl.ds(block * EACH, EACH), :]
        copies.append(pltpu.make_async_copy(source, conv_hbm.at[tap, :, :, lanes], sems.at[block]))
    source = rows.at[:, pl.ds(CONV_ROWS, PROJ_ROWS), :]
    copies.append(pltpu.make_async_copy(source, head_hbm.at[half], sems.at[HALF]))
    for copy in copies:
        copy.start()
    summed = rows[0, CHUNK:, :]
    for peer in range(1, PEERS):
        summed = summed + rows[peer, CHUNK:, :]
    if flip:
        gain_sum = refs[7]
        gain_sum[...] = (summed + gain_before[...])[0:wide, :]
        copies.append(pltpu.make_async_copy(gain_sum, gain_out, sems.at[HALF + 1]))
        copies[-1].start()
    else:
        gain_out[...] = summed
    for copy in copies:
        copy.wait()


def place(flip, places, rows, before=None):
    f32 = jnp.float32
    return pl.pallas_call(
        functools.partial(place_kernel, flip),
        in_specs=[IN_SMEM, IN_VMEM] + ([IN_VMEM, IN_HBM, IN_HBM] if flip else []),
        out_specs=[IN_HBM, IN_HBM, IN_HBM if flip else IN_VMEM],
        out_shape=(
            jax.ShapeDtypeStruct((TAPS, PEERS, EACH, C), f32),
            jax.ShapeDtypeStruct((2, PEERS, PROJ_ROWS, PROJ), f32),
            jax.ShapeDtypeStruct((C // 128 if flip else GAIN_ROWS, 128), f32),
        ),
        scratch_shapes=[DMA((HALF + 2,))] + ([VMEM((C // 128, 128), f32)] if flip else []),
        input_output_aliases={3: 0, 4: 1} if flip else {},
        compiler_params=pltpu.CompilerParams(vmem_limit_bytes=24 << 20),
        cost_estimate=pl.CostEstimate(flops=1 << 20, bytes_accessed=4 << 20, transcendentals=0),
        name="place_other" if flip else "place_mine",
    )(places, rows, *((before[2], before[0], before[1]) if flip else ()))


def body(segments, conv_weight, gain, head, group, positive):
    f32 = jnp.float32
    peers = ("zl", "yh", "yl", "x")
    swap = [(0, 1), (1, 0)]
    places = jnp.stack([lax.axis_index(("yh", "x")), lax.axis_index("core")]).astype(jnp.int32)
    normed, slope, pack, send = forward(group, positive, segments, conv_weight, gain.reshape(1, C), head)
    gathered = lax.all_to_all(send, ("yh", "x"), 0, 0)
    pack = jnp.where(places[1] >= 0, pack, 0.0)
    grad, keep, give = weight_gradient(places, gathered, pack, normed, slope)
    received = lax.ppermute(give, "core", swap)
    gain_part = gain_gradient(grad, segments, conv_weight)
    paired, gain_part = small_call(
        pair_sum_kernel,
        (jax.ShapeDtypeStruct((PEERS, CHUNK, 128), f32), jax.ShapeDtypeStruct((GAIN_ROWS, 128), f32)),
        "pair_sum",
        keep,
        received,
        gain_part,
    )
    across = lax.all_to_all(paired, peers, 0, 0)
    chunk = small_call(peer_sum_kernel, jax.ShapeDtypeStruct((LONG, 128), f32), "peer_sum", across, gain_part)
    rings = [lax.ppermute(chunk, "zh", [(i, (i + d) % STACKS) for i in range(STACKS)]) for d in (1, 2, 3)]
    spread = small_call(
        stack_sum_kernel, jax.ShapeDtypeStruct((PEERS, LONG, 128), f32), "stack_sum", chunk, *rings
    )
    mine = lax.all_to_all(spread, peers, 0, 0)
    other = lax.ppermute(mine, "core", swap)
    conv_grad, head_grad, gain_grad = place(True, places, other, place(False, places, mine))
    return conv_grad.reshape(TAPS, C, C), gain_grad.reshape(C), head_grad.reshape(C, PROJ)


def solution(mesh):
    fine = Mesh(mesh.devices.reshape(4, 2, 4, 2, 2, 2), ("x", "yh", "zh", "zl", "yl", "core"))
    row, grp = ("x", "yh"), ("zh", "zl", "yl", "core")
    placed = (P(grp, row, None, None), P(), P(), P(), P(grp, row), P(grp, row))
    return jax.shard_map(body, mesh=fine, in_specs=placed, out_specs=(P(), P(), P()), check_vma=False)
```
